512 devices in a mesh: bank: 8 (over x, core), gal: 64 (over z, y).
Axes of the slice: x: 4, y: 8, z: 8, core: 2. Of those that a mesh axis runs over, the one named last changes fastest.
Arguments:
- bank_queries: bfloat16 [4096, 768], P(('bank', 'gal'))
- gallery: bfloat16 [262144, 768], P('gal')
- test_queries: bfloat16 [2048, 768], P(('bank', 'gal'))
- test_slabs: int32 [2048, 8], P('bank'), may hold values from 0 to 63, all different within a row; in each aligned block of 4 rows (0 to 3, 4 to 7, ...) at most 2 rows name the same one
- test_offsets: int32 [2048, 8], P('bank'), may hold values from 0 to 31
Outputs:
- pooled: float32 [2048, 768], P(('bank', 'gal'))
The draws below stay inside these ranges and needn't reach their ends.
Inputs may be any that keep to these rules, and one draw needn't show every extreme that they name: `test_slabs`: each row names 8 different slabs; the 4 rows of one device name no slab more than 2 times, and on some devices one slab exactly 2 times.
All inputs are finite; a program needn't handle non-finite values.
Results may differ from the reference program's by a relative error of at most 0.0065.
Values may be sent and summed in bfloat16 or wider, within the bound.
A program may use at most 64 MiB of HBM per device.

```python
import math
import jax
import jax.numpy as jnp
import numpy as np
from jax import lax

D = 768
BLOCK = 128
NLIST = 8
ROUTE_CAP = 2
GAL_DEV = 4096
TQ_DEV = 4
NGAL = 262144
BANKQ = 4096
TQUERIES = 2048
N_GAL = 64


centre_count = 256


copy_noise = 0.3


def embed_rows(shared_key, row_key, positions):
    centres = jax.random.normal(jax.random.fold_in(shared_key, 3), (centre_count, D), jnp.float32)
    direction = jax.random.normal(jax.random.fold_in(shared_key, 5), (D,), jnp.float32)

    def one_row(position):
        pieces = jax.random.split(jax.random.fold_in(row_key, position), 4)
        alignment = jax.random.uniform(pieces[0], (), jnp.float32, -1.0, 1.0)
        loading = jax.random.uniform(pieces[1], (), jnp.float32, 0.2, 1.2)
        cluster = jax.random.randint(pieces[2], (), 0, centre_count)
        noise_part = jax.random.normal(pieces[3], (D,), jnp.float32)
        spread = jnp.float32(1.0)
        base_row = alignment * direction + loading * centres[cluster] + 0.8 * noise_part
        return (base_row, spread)
    return jax.vmap(one_row)(positions)


def draw_gallery(key, part):
    base_rows, spread = embed_rows(jax.random.fold_in(key, 101), jax.random.fold_in(key, 111), jnp.arange(NGAL, dtype=jnp.int32))
    return (base_rows * spread[:, None]).astype(jnp.bfloat16)


def draw_bank_queries(key, part):
    shared_key = jax.random.fold_in(key, 101)
    targets = jax.random.randint(jax.random.fold_in(key, 211), (BANKQ,), 0, NGAL)
    copied = jax.random.randint(jax.random.fold_in(key, 212), (BANKQ, 1), 0, 2).astype(jnp.float32)
    hub_rows, unused = embed_rows(shared_key, jax.random.fold_in(key, 111), targets)
    fresh_rows, spread = embed_rows(shared_key, jax.random.fold_in(key, 222), jnp.arange(BANKQ, dtype=jnp.int32))
    noise_part = jax.random.normal(jax.random.fold_in(key, 223), (BANKQ, D), jnp.float32)
    near_rows = hub_rows + copy_noise * noise_part
    mixed = copied * near_rows + (1.0 - copied) * fresh_rows
    return (mixed * spread[:, None]).astype(jnp.bfloat16)


def draw_test_queries(key, part):
    base_rows, spread = embed_rows(jax.random.fold_in(key, 101), jax.random.fold_in(key, 333), jnp.arange(TQUERIES, dtype=jnp.int32))
    return (base_rows * spread[:, None]).astype(jnp.bfloat16)


def place_ends(values, stream_key, smallest, largest):
    index_at = [jax.random.randint(jax.random.fold_in(stream_key, axis), (), 0, length) for axis, length in enumerate(values.shape)]
    main_axis = values.shape.index(max(values.shape))
    next_to = index_at[:main_axis] + [(index_at[main_axis] + 1) % values.shape[main_axis]] + index_at[main_axis + 1:]
    return values.at[tuple(index_at)].set(smallest).at[tuple(next_to)].set(largest)


def deal_out(rng, own, number, rows, amount, top, bound, slope):
    order = jax.random.permutation(rng, amount)
    packed, common = portions_of(amount, rows * top, bound, slope, True), portions_of(amount, rows * top, bound, slope, False)
    places = jnp.arange(amount)

    def named(tallies, rotation):
        used = int((tallies > 0).sum())
        fixed = max(1, used // 4)
        passed = fixed + (places - fixed + rotation * (used - fixed)) % max(1, amount - fixed)
        return jnp.zeros((amount,), jnp.int32).at[order[jnp.where(places < fixed, places, passed)]].set(jnp.asarray(tallies, jnp.int32))

    tallies = jnp.where(number % 4 == 0, named(packed, number // 4), named(common, number - number // 4 - 1))
    mixed = jax.random.permutation(jax.random.fold_in(own, 3), amount)
    donor, taker = mixed[0:amount // 2 * 2:2], mixed[1:amount // 2 * 2:2]
    room = jnp.minimum(tallies[donor] - 1, bound - tallies[taker]) // 2
    room = jnp.where((donor == order[0]) | (taker == order[0]) | (tallies[taker] == 0), 0, jnp.maximum(room, 0))
    passed = jax.random.randint(jax.random.fold_in(own, 4), (amount // 2,), 0, 1 << 20) % (room + 1)
    tallies = tallies.at[donor].add(-passed).at[taker].add(passed)
    members = jnp.searchsorted(jnp.cumsum(tallies), jnp.arange(rows * top), side="right").astype(jnp.int32)
    grid = members.reshape(top, rows).T
    grid = grid[jax.random.permutation(jax.random.fold_in(own, 1), rows)]
    rotation = jax.random.randint(jax.random.fold_in(own, 2), (rows, 1), 0, top)
    return jnp.take_along_axis(grid, (jnp.arange(top)[None, :] + rotation) % top, axis=1)


def portions_of(amount, total, reach, lean, full):
    weights = [(1 << 20) // math.isqrt(standing ** lean) + 1 for standing in range(1, amount + 1)]
    largest = reach if full else min(reach, max(-(-total // amount), total * weights[0] // sum(weights)))
    least = 1 if total - largest >= amount - 1 else 0
    holding, surplus = [largest] + [least] * (amount - 1), total - largest - least * (amount - 1)
    while surplus > 0:
        movable = [i for i in range(1, amount) if holding[i] < largest] or [i for i in range(1, amount) if holding[i] < reach]
        whole, left = sum([weights[i] for i in movable]), surplus
        for i in movable:
            extra = min(reach - holding[i], max(1, left * weights[i] // whole), surplus)
            holding[i] = holding[i] + extra
            surplus = surplus - extra
    return np.array(holding)


def setup_inputs(seed: int = 0) -> dict:
    seeds = jax.random.split(jax.random.key(seed), 6)
    bank_queries = draw_bank_queries(jax.random.fold_in(seeds[5], 71), 0)
    gallery = draw_gallery(jax.random.fold_in(seeds[5], 71), 0)
    test_queries = draw_test_queries(jax.random.fold_in(seeds[5], 71), 0)
    test_slabs_keys = jax.random.split(jax.random.fold_in(seeds[3], 1), TQUERIES // TQ_DEV)
    test_slabs_turns = jax.random.permutation(jax.random.fold_in(seeds[3], 3), TQUERIES // TQ_DEV)
    test_slabs = jax.vmap(lambda own, number: deal_out(jax.random.fold_in(seeds[3], 2), own, number, TQ_DEV, N_GAL, NLIST, ROUTE_CAP, 2))(test_slabs_keys, test_slabs_turns).reshape((TQUERIES, NLIST))
    test_offsets = place_ends(jax.random.randint(seeds[4], (TQUERIES, NLIST), 0, GAL_DEV // BLOCK), jax.random.fold_in(seeds[4], 1), 0, (GAL_DEV // BLOCK) - 1).astype(jnp.int32)
    return dict(bank_queries=bank_queries, gallery=gallery, test_queries=test_queries, test_slabs=test_slabs, test_offsets=test_offsets)


SHARPNESS = 20.0
epsilon = 1e-06

def row_scale(matrix):
    values = matrix.astype(jnp.float32)
    return lax.rsqrt(lax.optimization_barrier(jnp.sum(values * values, axis=1)) + epsilon)

def reference(bank_queries, gallery, test_queries, test_slabs, test_offsets):
    gallery_scale = row_scale(gallery)
    bank_scale = row_scale(bank_queries)
    test_scale = row_scale(test_queries)
    slab_rows = gallery.reshape(N_GAL, GAL_DEV, D)
    slab_scale = gallery_scale.reshape(N_GAL, GAL_DEV)

    def column_slab(inputs):
        rows_here, scale_here = inputs
        products = jnp.dot(bank_queries, rows_here.T, preferred_element_type=jnp.float32)
        scores = SHARPNESS * products * bank_scale[:, None] * scale_here[None, :]
        return lax.optimization_barrier(jnp.sum(jnp.exp(scores), axis=0))
    colsum = lax.map(column_slab, (slab_rows, slab_scale))
    log_col = jnp.log(colsum)
    blocks_here = GAL_DEV // BLOCK

    def test_slab(running_sums, inputs):
        numerator, denominator = running_sums
        rows_here, scale_here, logc_here, slab_index = inputs
        local_blocks = jnp.arange(blocks_here, dtype=jnp.int32)
        block_hits = (test_slabs == slab_index)[:, :, None] & (test_offsets[:, :, None] == local_blocks[None, None, :])
        listed = jnp.any(block_hits, axis=1)
        row_mask = jnp.repeat(listed, BLOCK, axis=1)
        products = jnp.dot(test_queries, rows_here.T, preferred_element_type=jnp.float32)
        logits = SHARPNESS * products * test_scale[:, None] * scale_here[None, :] - logc_here[None, :]
        weights = jnp.where(row_mask, jnp.exp(logits), jnp.float32(0.0))
        denominator = denominator + lax.optimization_barrier(jnp.sum(weights, axis=1))
        numerator = numerator + jnp.dot(weights.astype(jnp.bfloat16), rows_here, preferred_element_type=jnp.float32)
        return ((numerator, denominator), None)
    start_sums = (jnp.zeros((TQUERIES, D), jnp.float32), jnp.zeros((TQUERIES,), jnp.float32))
    (numerator, denominator), unused = lax.scan(test_slab, start_sums, (slab_rows, slab_scale, log_col, jnp.arange(N_GAL, dtype=jnp.int32)))
    return numerator / denominator[:, None]
```

```python
import functools
import jax
import jax.numpy as jnp
from jax import lax
from jax.experimental import pallas as pl
from jax.experimental.pallas import tpu as pltpu
from jax.sharding import PartitionSpec as P

BLOCK = 128
SLOTS = 2
EXTRA = 128
SHARPNESS = 20.0
LOG2E = 1.4426950408889634
epsilon = 1e-06
MESH = pl.DeviceIdType.MESH
NT = (((1,), (1,)), ((), ()))
NN = (((1,), (0,)), ((), ()))


def matmul(left, right, dims):
    return lax.dot_general(left, right, dims, preferred_element_type=jnp.float32)


def kernel(
    n_bank, n_z, n_y, chunk,
    bankq_ref, testq_ref, slabs_ref, offsets_ref, gal_hbm,
    out_ref,
    gal, bank_all, test_all, gscale, sums, scores, back_out, back_in,
    gal_sem, hop_send, hop_recv, sum_send, sum_recv, back_send, back_recv,
):
    n_gal = n_z * n_y
    rows, width = gal.shape
    half = width // 2
    chunks = rows // chunk
    me_b = lax.axis_index("bank")
    me_g = lax.axis_index("gal")
    me_z = me_g // n_y
    me_y = me_g % n_y

    def load(n):
        part = pl.ds(n * chunk, chunk)
        return pltpu.make_async_copy(gal_hbm.at[part], gal.at[part], gal_sem.at[n])

    for n in range(chunks):
        load(n).start()

    barrier = pltpu.get_barrier_semaphore()

    def greet_gal(k, carry):
        pl.semaphore_signal(
            barrier, inc=1, device_id={"gal": (me_g + k) % n_gal}, device_id_type=MESH
        )
        return carry

    def greet_bank(k, carry):
        pl.semaphore_signal(
            barrier, inc=1, device_id={"bank": (me_b + k) % n_bank}, device_id_type=MESH
        )
        return carry

    lax.fori_loop(1, n_gal, greet_gal, 0)
    lax.fori_loop(1, n_bank, greet_bank, 0)
    pl.semaphore_wait(barrier, n_gal + n_bank - 2)

    gathers = ((bankq_ref, bank_all), (testq_ref, test_all))
    left, right = pl.ds(0, half), pl.ds(half, half)

    def first(t, side, k):
        own, full = gathers[t]
        cols = (left, right)[side]
        if side == 0:
            peer = me_z * n_y + (me_y + k) % n_y
        else:
            peer = (me_z + k) % n_z * n_y + me_y
        return pltpu.make_async_remote_copy(
            src_ref=own.at[:, cols],
            dst_ref=full.at[me_z, me_y, :, cols],
            send_sem=hop_send.at[t, side, 0, k],
            recv_sem=hop_recv.at[t, side, 0, k],
            device_id={"gal": peer},
            device_id_type=MESH,
        )

    def second(t, side, k):
        full = gathers[t][1]
        if side == 0:
            peer = (me_z + k) % n_z * n_y + me_y
            part = full.at[me_z, :, :, left]
        else:
            peer = me_z * n_y + (me_y + k) % n_y
            part = full.at[:, me_y, :, right]
        return pltpu.make_async_remote_copy(
            src_ref=part,
            dst_ref=part,
            send_sem=hop_send.at[t, side, 1, k],
            recv_sem=hop_recv.at[t, side, 1, k],
            device_id={"gal": peer},
            device_id_type=MESH,
        )

    spans = ((n_y, n_z), (n_z, n_y))
    for t in range(2):
        for side in range(2):
            for k in range(1, spans[side][0]):
                first(t, side, k).start()
    bank_all[me_z, me_y] = bankq_ref[...]
    test_all[me_z, me_y] = testq_ref[...]

    ones = jnp.ones((8, width), jnp.bfloat16)

    def norms(n, carry):
        load(n).wait()
        part = pl.ds(pl.multiple_of(n * chunk, chunk), chunk)
        values = gal[part, :].astype(jnp.float32)
        squares = values * values
        high = squares.astype(jnp.bfloat16)
        low = (squares - high.astype(jnp.float32)).astype(jnp.bfloat16)
        total = matmul(ones, high, NT) + matmul(ones, low, NT)
        gscale[:, part] = lax.rsqrt(total[0:1] + epsilon)
        return carry

    lax.fori_loop(0, chunks, norms, 0)

    for t in range(2):
        for side in range(2):
            for k in range(1, spans[side][0]):
                first(t, side, k).wait_recv()
            for k in range(1, spans[side][1]):
                second(t, side, k).start()

    slots = SLOTS * n_gal
    own_rows = testq_ref.shape[0]
    queries = n_gal * own_rows
    slabs = slabs_ref[...]
    offsets = offsets_ref[...].astype(jnp.float32)
    named = slabs == me_g
    hit = jnp.sum(jnp.where(named, 1.0, 0.0), axis=0, keepdims=True)
    place = jnp.sum(jnp.where(named, offsets, 0.0), axis=0, keepdims=True)
    hit8 = jnp.broadcast_to(hit, (8, queries))
    lane = lax.broadcasted_iota(jnp.int32, (8, queries), 1) % own_rows
    rank8 = jnp.zeros((8, queries), jnp.float32)
    for k in range(1, own_rows):
        rank8 = rank8 + jnp.where(lane >= k, pltpu.roll(hit8, k, 1), 0.0)
    rank = rank8[0:1]
    slot_row = lax.broadcasted_iota(jnp.int32, (slots, queries), 0)
    query_col = lax.broadcasted_iota(jnp.int32, (slots, queries), 1)
    pick = jnp.where(
        (query_col // own_rows == slot_row // SLOTS)
        & (hit > 0.5)
        & (rank.astype(jnp.int32) == slot_row % SLOTS),
        1.0,
        0.0,
    )
    slot_hit = jnp.sum(pick, axis=1, keepdims=True)
    slot_place = jnp.sum(pick * place, axis=1, keepdims=True)
    slot_block = jnp.where(slot_hit > 0.5, slot_place, -1.0).astype(jnp.int32)

    for side in range(2):
        for k in range(1, spans[side][1]):
            second(0, side, k).wait_recv()
    portion = bank_all[...].reshape(n_gal * bankq_ref.shape[0], width)
    values = portion.astype(jnp.float32)
    bank_scale = (SHARPNESS * LOG2E) * lax.rsqrt(
        jnp.sum(values * values, axis=1, keepdims=True) + epsilon
    )

    def column_sums(n, carry):
        part = pl.ds(pl.multiple_of(n * chunk, chunk), chunk)
        s = matmul(portion, gal[part, :], NT)
        e = jnp.exp2(s * bank_scale * gscale[:, part])
        sums[me_b, :, part] = jnp.sum(e, axis=0, keepdims=True)
        return carry

    lax.fori_loop(0, chunks, column_sums, 0)

    def share(k):
        return pltpu.make_async_remote_copy(
            src_ref=sums.at[me_b],
            dst_ref=sums.at[me_b],
            send_sem=sum_send.at[k],
            recv_sem=sum_recv.at[k],
            device_id={"bank": (me_b + k) % n_bank},
            device_id_type=MESH,
        )

    for k in range(1, n_bank):
        share(k).start()

    for side in range(2):
        for k in range(1, spans[side][1]):
            second(1, side, k).wait_recv()
    asked = matmul(
        pick.astype(jnp.bfloat16), test_all[...].reshape(queries, width), NN
    )
    test_scale = (SHARPNESS * LOG2E) * lax.rsqrt(
        jnp.sum(asked * asked, axis=1, keepdims=True) + epsilon
    )
    asked = asked.astype(jnp.bfloat16)

    def raw_weights(n, carry):
        part = pl.ds(pl.multiple_of(n * chunk, chunk), chunk)
        s = matmul(asked, gal[part, :], NT)
        e = jnp.exp2(s * test_scale * gscale[:, part])
        block = n * (chunk // BLOCK) + (
            lax.broadcasted_iota(jnp.int32, (slots, chunk), 1) // BLOCK
        )
        scores[:, part] = jnp.where(block == slot_block, e, 0.0)
        return carry

    lax.fori_loop(0, chunks, raw_weights, 0)

    for k in range(1, n_bank):
        share(k).wait_recv()
    inverse = 1.0 / jnp.sum(sums[...], axis=0)

    weights = scores[...] * inverse
    total = jnp.sum(weights, axis=1, keepdims=True)
    numer = matmul(weights.astype(jnp.bfloat16), gal[...], NN)
    total_high = total.astype(jnp.bfloat16).astype(jnp.float32)
    lanes = lax.broadcasted_iota(jnp.int32, (slots, EXTRA), 1)
    extra = jnp.where(lanes == 0, total_high, jnp.where(lanes == 1, total - total_high, 0.0))
    message = jnp.concatenate([numer, extra], axis=1).astype(jnp.bfloat16)
    back_out[...] = message.reshape(n_gal, SLOTS, width + EXTRA)

    def give(k, carry):
        peer = (me_g + k) % n_gal
        pltpu.make_async_remote_copy(
            src_ref=back_out.at[peer],
            dst_ref=back_in.at[me_g],
            send_sem=back_send,
            recv_sem=back_recv,
            device_id={"gal": peer},
            device_id_type=MESH,
        ).start()
        return carry

    lax.fori_loop(1, n_gal, give, 0)
    back_in[me_g] = back_out[me_g]

    slab_of = lax.broadcasted_iota(jnp.int32, (slots, queries), 0) // SLOTS
    lists = jnp.zeros((slots, queries), jnp.float32)
    for s in range(slabs_ref.shape[0]):
        lists = lists + jnp.where(slabs[s : s + 1] == slab_of, 1.0, 0.0)
    own_row = lax.broadcasted_iota(jnp.int32, (8, queries), 0)
    own_col = lax.broadcasted_iota(jnp.int32, (8, queries), 1)
    mine = jnp.where(
        (own_col == me_g * own_rows + own_row) & (own_row < own_rows), 1.0, 0.0
    )
    mine_lists = matmul(mine.astype(jnp.bfloat16), lists.astype(jnp.bfloat16), NT)
    before = jnp.where(
        lax.broadcasted_iota(jnp.int32, (8, 8), 1) < lax.broadcasted_iota(jnp.int32, (8, 8), 0),
        1.0,
        0.0,
    )
    mine_rank = matmul(before, mine_lists, NN)
    slot_col = lax.broadcasted_iota(jnp.int32, (8, slots), 1)
    take = jnp.where(
        (mine_lists > 0.5) & ((mine_rank + 0.5).astype(jnp.int32) == slot_col % SLOTS), 1.0, 0.0
    )

    everyone = pltpu.make_async_remote_copy(
        src_ref=back_out.at[pl.ds(0, n_gal - 1)],
        dst_ref=back_in.at[pl.ds(0, n_gal - 1)],
        send_sem=back_send,
        recv_sem=back_recv,
        device_id={"gal": (me_g + 1) % n_gal},
        device_id_type=MESH,
    )
    everyone.wait_recv()
    got = back_in[...].reshape(slots, width + EXTRA)
    answer = matmul(take.astype(jnp.bfloat16), got, NN)
    bottom = answer[:, width : width + 1] + answer[:, width + 1 : width + 2]
    out_ref[...] = (answer[:, :width] / bottom)[:own_rows]

    everyone.wait_send()
    for k in range(1, n_bank):
        share(k).wait_send()
    for t in range(2):
        for side in range(2):
            for k in range(1, spans[side][0]):
                first(t, side, k).wait_send()
            for k in range(1, spans[side][1]):
                second(t, side, k).wait_send()


def body(n_bank, n_z, n_y, chunk, bank_queries, gallery, test_queries, test_slabs, test_offsets):
    rows, width = gallery.shape
    n_gal = n_z * n_y
    own_bank, own_test = bank_queries.shape[0], test_queries.shape[0]
    slots = SLOTS * n_gal
    hops = (2, 2, 2, max(n_z, n_y))
    vmem = pl.BlockSpec(memory_space=pltpu.VMEM)
    return pl.pallas_call(
        functools.partial(kernel, n_bank, n_z, n_y, chunk),
        out_shape=jax.ShapeDtypeStruct((own_test, width), jnp.float32),
        in_specs=[vmem] * 4 + [pl.BlockSpec(memory_space=pl.ANY)],
        out_specs=vmem,
        scratch_shapes=[
            pltpu.VMEM((rows, width), jnp.bfloat16),
            pltpu.VMEM((n_z, n_y, own_bank, width), jnp.bfloat16),
            pltpu.VMEM((n_z, n_y, own_test, width), jnp.bfloat16),
            pltpu.VMEM((1, rows), jnp.float32),
            pltpu.VMEM((n_bank, 1, rows), jnp.float32),
            pltpu.VMEM((slots, rows), jnp.float32),
            pltpu.VMEM((n_gal, SLOTS, width + EXTRA), jnp.bfloat16),
            pltpu.VMEM((n_gal, SLOTS, width + EXTRA), jnp.bfloat16),
            pltpu.SemaphoreType.DMA((rows // chunk,)),
            pltpu.SemaphoreType.DMA(hops),
            pltpu.SemaphoreType.DMA(hops),
            pltpu.SemaphoreType.DMA((n_bank,)),
            pltpu.SemaphoreType.DMA((n_bank,)),
            pltpu.SemaphoreType.DMA,
            pltpu.SemaphoreType.DMA,
        ],
        compiler_params=pltpu.CompilerParams(
            collective_id=0, has_side_effects=True, vmem_limit_bytes=48 * 1024 * 1024
        ),
    )(bank_queries, test_queries, test_slabs.T, test_offsets.T, gallery)


def solution(mesh):
    n_bank, n_gal = mesh.shape["bank"], mesh.shape["gal"]
    n_z = 8 if n_gal == 64 else 2
    run = functools.partial(body, n_bank, n_z, n_gal // n_z, 512)
    in_specs = (
        P(("bank", "gal"), None),
        P("gal", None),
        P(("bank", "gal"), None),
        P("bank", None),
        P("bank", None),
    )
    out_specs = P(("bank", "gal"), None)
    return jax.shard_map(run, mesh=mesh, in_specs=in_specs, out_specs=out_specs, check_vma=False)
```

```python
import functools
import jax
import jax.numpy as jnp
from jax import lax
from jax.experimental import pallas as pl
from jax.experimental.pallas import tpu as pltpu
from jax.sharding import PartitionSpec as P

BLOCK = 128
SLOTS = 2
EXTRA = 128
SHARPNESS = 20.0
LOG2E = 1.4426950408889634
epsilon = 1e-06
MESH = pl.DeviceIdType.MESH
NT = (((1,), (1,)), ((), ()))
NN = (((1,), (0,)), ((), ()))


def matmul(left, right, dims):
    return lax.dot_general(left, right, dims, preferred_element_type=jnp.float32)


def kernel(
    n_bank, n_z, n_y, chunk,
    bankq_hbm, testq_hbm, slabs_hbm, offsets_hbm, gal_hbm,
    out_ref,
    slabs_ref, offsets_ref, gal, bank_all, test_all, gscale, sums, scores, back_out, back_in,
    own_sem, gal_sem, hop_send, hop_recv, sum_send, sum_recv, back_send, back_recv,
):
    n_gal = n_z * n_y
    rows, width = gal.shape
    half = width // 2
    chunks = rows // chunk
    me_b = lax.axis_index("bank")
    me_g = lax.axis_index("gal")
    me_z = me_g // n_y
    me_y = me_g % n_y

    def load(n):
        part = pl.ds(n * chunk, chunk)
        return pltpu.make_async_copy(gal_hbm.at[part], gal.at[part], gal_sem.at[n])

    barrier = pltpu.get_barrier_semaphore()

    def far_first(n):
        return sorted(range(1, n), key=lambda k: -min(k, n - k))

    def ring_peer(axis, k):
        if axis == 0:
            return me_z * n_y + (me_y + k) % n_y
        return (me_z + k) % n_z * n_y + me_y

    for axis, n in ((0, n_y), (1, n_z)):
        for k in far_first(n):
            pl.semaphore_signal(
                barrier, inc=1, device_id={"gal": ring_peer(axis, k)}, device_id_type=MESH
            )
    for k in range(1, n_bank):
        pl.semaphore_signal(
            barrier, inc=1, device_id={"bank": (me_b + k) % n_bank}, device_id_type=MESH
        )
    fetches = [
        pltpu.make_async_copy(bankq_hbm, bank_all.at[me_z, me_y], own_sem.at[0]),
        pltpu.make_async_copy(testq_hbm, test_all.at[me_z, me_y], own_sem.at[1]),
        pltpu.make_async_copy(slabs_hbm, slabs_ref, own_sem.at[2]),
        pltpu.make_async_copy(offsets_hbm, offsets_ref, own_sem.at[3]),
    ]
    for fetch in fetches:
        fetch.start()
    for n in range(chunks):
        load(n).start()
    pl.semaphore_wait(barrier, n_y + n_z + n_bank - 3)

    gathers = ((bankq_hbm, bank_all), (testq_hbm, test_all))
    left, right = pl.ds(0, half), pl.ds(half, half)

    def first(t, side, k):
        own, full = gathers[t]
        cols = (left, right)[side]
        return pltpu.make_async_remote_copy(
            src_ref=own.at[:, cols],
            dst_ref=full.at[me_z, me_y, :, cols],
            send_sem=hop_send.at[t, side, 0, k],
            recv_sem=hop_recv.at[t, side, 0, k],
            device_id={"gal": ring_peer(side, k)},
            device_id_type=MESH,
        )

    def second(t, side, k):
        full = gathers[t][1]
        if side == 0:
            part = full.at[me_z, :, :, left]
        else:
            part = full.at[:, me_y, :, right]
        return pltpu.make_async_remote_copy(
            src_ref=part,
            dst_ref=part,
            send_sem=hop_send.at[t, side, 1, k],
            recv_sem=hop_recv.at[t, side, 1, k],
            device_id={"gal": ring_peer(1 - side, k)},
            device_id_type=MESH,
        )

    spans = ((n_y, n_z), (n_z, n_y))
    for t in range(2):
        for side in range(2):
            for k in far_first(spans[side][0]):
                first(t, side, k).start()

    ones = jnp.ones((8, width), jnp.bfloat16)

    def norms(n, carry):
        load(n).wait()
        part = pl.ds(pl.multiple_of(n * chunk, chunk), chunk)
        values = gal[part, :].astype(jnp.float32)
        squares = values * values
        high = squares.astype(jnp.bfloat16)
        low = (squares - high.astype(jnp.float32)).astype(jnp.bfloat16)
        total = matmul(ones, high, NT) + matmul(ones, low, NT)
        gscale[:, part] = lax.rsqrt(total[0:1] + epsilon)
        return carry

    lax.fori_loop(0, chunks, norms, 0, unroll=True)

    for fetch in fetches:
        fetch.wait()
    for t in range(2):
        for side in range(2):
            for k in range(1, spans[side][0]):
                first(t, side, k).wait_recv()
            for k in far_first(spans[side][1]):
                second(t, side, k).start()

    slots = SLOTS * n_gal
    own_rows = testq_hbm.shape[0]
    queries = n_gal * own_rows
    slabs = slabs_ref[...]
    offsets = offsets_ref[...].astype(jnp.float32)
    named = slabs == me_g
    hit = jnp.sum(jnp.where(named, 1.0, 0.0), axis=0, keepdims=True)
    place = jnp.sum(jnp.where(named, offsets, 0.0), axis=0, keepdims=True)
    hit8 = jnp.broadcast_to(hit, (8, queries))
    lane = lax.broadcasted_iota(jnp.int32, (8, queries), 1) % own_rows
    rank8 = jnp.zeros((8, queries), jnp.float32)
    for k in range(1, own_rows):
        rank8 = rank8 + jnp.where(lane >= k, pltpu.roll(hit8, k, 1), 0.0)
    rank = rank8[0:1]
    slot_row = lax.broadcasted_iota(jnp.int32, (slots, queries), 0)
    query_col = lax.broadcasted_iota(jnp.int32, (slots, queries), 1)
    pick = jnp.where(
        (query_col // own_rows == slot_row // SLOTS)
        & (hit > 0.5)
        & (rank.astype(jnp.int32) == slot_row % SLOTS),
        1.0,
        0.0,
    )
    slot_hit = jnp.sum(pick, axis=1, keepdims=True)
    slot_place = jnp.sum(pick * place, axis=1, keepdims=True)
    slot_block = jnp.where(slot_hit > 0.5, slot_place, -1.0).astype(jnp.int32)

    for side in range(2):
        for k in range(1, spans[side][1]):
            second(0, side, k).wait_recv()
    portion = bank_all[...].reshape(n_gal * bankq_hbm.shape[0], width)
    values = portion.astype(jnp.float32)
    bank_scale = (SHARPNESS * LOG2E) * lax.rsqrt(
        jnp.sum(values * values, axis=1, keepdims=True) + epsilon
    )

    def column_sums(n, carry):
        part = pl.ds(pl.multiple_of(n * chunk, chunk), chunk)
        s = matmul(portion, gal[part, :], NT)
        e = jnp.exp2(s * bank_scale * gscale[:, part])
        sums[me_b, :, part] = jnp.sum(e, axis=0, keepdims=True)
        return carry

    lax.fori_loop(0, chunks, column_sums, 0, unroll=True)

    def share(k):
        return pltpu.make_async_remote_copy(
            src_ref=sums.at[me_b],
            dst_ref=sums.at[me_b],
            send_sem=sum_send.at[k],
            recv_sem=sum_recv.at[k],
            device_id={"bank": (me_b + k) % n_bank},
            device_id_type=MESH,
        )

    for k in range(1, n_bank):
        share(k).start()

    for side in range(2):
        for k in range(1, spans[side][1]):
            second(1, side, k).wait_recv()
    asked = matmul(
        pick.astype(jnp.bfloat16), test_all[...].reshape(queries, width), NN
    )
    test_scale = (SHARPNESS * LOG2E) * lax.rsqrt(
        jnp.sum(asked * asked, axis=1, keepdims=True) + epsilon
    )
    asked = asked.astype(jnp.bfloat16)

    def raw_weights(n, carry):
        part = pl.ds(pl.multiple_of(n * chunk, chunk), chunk)
        s = matmul(asked, gal[part, :], NT)
        e = jnp.exp2(s * test_scale * gscale[:, part])
        block = n * (chunk // BLOCK) + (
            lax.broadcasted_iota(jnp.int32, (slots, chunk), 1) // BLOCK
        )
        scores[:, part] = jnp.where(block == slot_block, e, 0.0)
        return carry

    lax.fori_loop(0, chunks, raw_weights, 0, unroll=True)

    for k in range(1, n_bank):
        share(k).wait_recv()
    inverse = 1.0 / jnp.sum(sums[...], axis=0)

    weights = scores[...] * inverse
    total = jnp.sum(weights, axis=1, keepdims=True)
    numer = matmul(weights.astype(jnp.bfloat16), gal[...], NN)
    total_high = total.astype(jnp.bfloat16).astype(jnp.float32)
    lanes = lax.broadcasted_iota(jnp.int32, (slots, EXTRA), 1)
    extra = jnp.where(lanes == 0, total_high, jnp.where(lanes == 1, total - total_high, 0.0))
    message = jnp.concatenate([numer, extra], axis=1).astype(jnp.bfloat16)
    back_out[...] = message.reshape(n_gal, SLOTS, width + EXTRA)

    def give(k, carry):
        step_z, step_y = k // n_y, k % n_y
        shift_z = n_z // 2 + jnp.where(step_z % 2 == 1, 1, n_z - 1) * ((step_z + 1) // 2)
        shift_y = n_y // 2 + jnp.where(step_y % 2 == 1, 1, n_y - 1) * ((step_y + 1) // 2)
        peer = (me_z + shift_z) % n_z * n_y + (me_y + shift_y) % n_y
        pltpu.make_async_remote_copy(
            src_ref=back_out.at[peer],
            dst_ref=back_in.at[me_g],
            send_sem=back_send,
            recv_sem=back_recv,
            device_id={"gal": peer},
            device_id_type=MESH,
        ).start()
        return carry

    lax.fori_loop(0, n_gal - 1, give, 0)
    back_in[me_g] = back_out[me_g]

    slab_of = lax.broadcasted_iota(jnp.int32, (slots, queries), 0) // SLOTS
    lists = jnp.zeros((slots, queries), jnp.float32)
    for s in range(slabs_ref.shape[0]):
        lists = lists + jnp.where(slabs[s : s + 1] == slab_of, 1.0, 0.0)
    own_row = lax.broadcasted_iota(jnp.int32, (8, queries), 0)
    own_col = lax.broadcasted_iota(jnp.int32, (8, queries), 1)
    mine = jnp.where(
        (own_col == me_g * own_rows + own_row) & (own_row < own_rows), 1.0, 0.0
    )
    mine_lists = matmul(mine.astype(jnp.bfloat16), lists.astype(jnp.bfloat16), NT)
    before = jnp.where(
        lax.broadcasted_iota(jnp.int32, (8, 8), 1) < lax.broadcasted_iota(jnp.int32, (8, 8), 0),
        1.0,
        0.0,
    )
    mine_rank = matmul(before, mine_lists, NN)
    slot_col = lax.broadcasted_iota(jnp.int32, (8, slots), 1)
    take = jnp.where(
        (mine_lists > 0.5) & ((mine_rank + 0.5).astype(jnp.int32) == slot_col % SLOTS), 1.0, 0.0
    )

    everyone = pltpu.make_async_remote_copy(
        src_ref=back_out.at[pl.ds(0, n_gal - 1)],
        dst_ref=back_in.at[pl.ds(0, n_gal - 1)],
        send_sem=back_send,
        recv_sem=back_recv,
        device_id={"gal": (me_g + 1) % n_gal},
        device_id_type=MESH,
    )
    everyone.wait_recv()
    got = back_in[...].reshape(slots, width + EXTRA)
    answer = matmul(take.astype(jnp.bfloat16), got, NN)
    bottom = answer[:, width : width + 1] + answer[:, width + 1 : width + 2]
    out_ref[...] = (answer[:, :width] / bottom)[:own_rows]

    everyone.wait_send()
    for k in range(1, n_bank):
        share(k).wait_send()
    for t in range(2):
        for side in range(2):
            for k in range(1, spans[side][0]):
                first(t, side, k).wait_send()
            for k in range(1, spans[side][1]):
                second(t, side, k).wait_send()


def body(n_bank, n_z, n_y, chunk, bank_queries, gallery, test_queries, test_slabs, test_offsets):
    rows, width = gallery.shape
    n_gal = n_z * n_y
    own_bank, own_test = bank_queries.shape[0], test_queries.shape[0]
    slots = SLOTS * n_gal
    hops = (2, 2, 2, max(n_z, n_y))
    vmem = pl.BlockSpec(memory_space=pltpu.VMEM)
    return pl.pallas_call(
        functools.partial(kernel, n_bank, n_z, n_y, chunk),
        out_shape=jax.ShapeDtypeStruct((own_test, width), jnp.float32),
        in_specs=[pl.BlockSpec(memory_space=pltpu.HBM)] * 5,
        out_specs=vmem,
        scratch_shapes=[
            pltpu.VMEM(test_slabs.T.shape, jnp.int32),
            pltpu.VMEM(test_slabs.T.shape, jnp.int32),
            pltpu.VMEM((rows, width), jnp.bfloat16),
            pltpu.VMEM((n_z, n_y, own_bank, width), jnp.bfloat16),
            pltpu.VMEM((n_z, n_y, own_test, width), jnp.bfloat16),
            pltpu.VMEM((1, rows), jnp.float32),
            pltpu.VMEM((n_bank, 1, rows), jnp.float32),
            pltpu.VMEM((slots, rows), jnp.float32),
            pltpu.VMEM((n_gal, SLOTS, width + EXTRA), jnp.bfloat16),
            pltpu.VMEM((n_gal, SLOTS, width + EXTRA), jnp.bfloat16),
            pltpu.SemaphoreType.DMA((4,)),
            pltpu.SemaphoreType.DMA((rows // chunk,)),
            pltpu.SemaphoreType.DMA(hops),
            pltpu.SemaphoreType.DMA(hops),
            pltpu.SemaphoreType.DMA((n_bank,)),
            pltpu.SemaphoreType.DMA((n_bank,)),
            pltpu.SemaphoreType.DMA,
            pltpu.SemaphoreType.DMA,
        ],
        compiler_params=pltpu.CompilerParams(
            collective_id=0, has_side_effects=True, vmem_limit_bytes=60 * 1024 * 1024
        ),
    )(bank_queries, test_queries, test_slabs.T, test_offsets.T, gallery)


def solution(mesh):
    n_bank, n_gal = mesh.shape["bank"], mesh.shape["gal"]
    n_z = 8 if n_gal == 64 else 2
    run = functools.partial(body, n_bank, n_z, n_gal // n_z, 512)
    in_specs = (
        P(("bank", "gal"), None),
        P("gal", None),
        P(("bank", "gal"), None),
        P("bank", None),
        P("bank", None),
    )
    out_specs = P(("bank", "gal"), None)
    return jax.shard_map(run, mesh=mesh, in_specs=in_specs, out_specs=out_specs, check_vma=False)
```

```python
import functools
import jax
import jax.numpy as jnp
from jax import lax
from jax.experimental import pallas as pl
from jax.experimental.pallas import tpu as pltpu
from jax.sharding import PartitionSpec as P

BLOCK = 128
SLOTS = 2
EXTRA = 128
SHARPNESS = 20.0
LOG2E = 1.4426950408889634
epsilon = 1e-06
MESH = pl.DeviceIdType.MESH
NT = (((1,), (1,)), ((), ()))
NN = (((1,), (0,)), ((), ()))


def matmul(left, right, dims):
    return lax.dot_general(left, right, dims, preferred_element_type=jnp.float32)


def kernel(
    n_bank, n_a, n_b, chunk,
    bankq_hbm, testq_hbm, slabs_hbm, offsets_hbm, gal_hbm,
    out_ref,
    slabs_ref, offsets_ref, gal, bank_all, test_row, test_out, test_in,
    gscale, near_sums, sums, scores, back_out, back_in,
    own_sem, gal_sem, bank_send, bank_recv, test_send, test_recv,
    sum_send, sum_recv, back_send, back_recv,
):
    n_gal = n_a * n_b
    rows, width = gal.shape
    chunks = rows // chunk
    me_bank = lax.axis_index("bank")
    me_g = lax.axis_index("gal")
    core = me_bank % 2
    me_a = jnp.where(core == 0, me_g % n_a, me_g // n_b)
    me_b = jnp.where(core == 0, me_g // n_a, me_g % n_b)

    def device(a, b):
        return jnp.where(core == 0, b * n_a + a, a * n_b + b)

    def along_a(k):
        return device((me_a + k) % n_a, me_b)

    def along_b(k):
        return device(me_a, (me_b + k) % n_b)

    def far_first(n):
        return sorted(range(1, n), key=lambda k: -min(k, n - k))

    def load(n):
        part = pl.ds(n * chunk, chunk)
        return pltpu.make_async_copy(gal_hbm.at[part], gal.at[part], gal_sem.at[n])

    barrier = pltpu.get_barrier_semaphore()
    for along, n in ((along_a, n_a), (along_b, n_b)):
        for k in far_first(n):
            pl.semaphore_signal(barrier, inc=1, device_id={"gal": along(k)}, device_id_type=MESH)
    for k in far_first(n_bank):
        pl.semaphore_signal(
            barrier, inc=1, device_id={"bank": (me_bank + k) % n_bank}, device_id_type=MESH
        )
    order = sorted(range(n_b), key=lambda k: (min(k, n_b - k), k))
    place_of = {k: p for p, k in enumerate(order)}
    fetches = [
        pltpu.make_async_copy(bankq_hbm, bank_all.at[0, 0], own_sem.at[0]),
        pltpu.make_async_copy(testq_hbm, test_row.at[me_a], own_sem.at[1]),
        pltpu.make_async_copy(slabs_hbm, slabs_ref, own_sem.at[2]),
        pltpu.make_async_copy(offsets_hbm, offsets_ref, own_sem.at[3]),
    ]
    for fetch in fetches:
        fetch.start()
    for n in range(chunks):
        load(n).start()
    pl.semaphore_wait(barrier, n_a + n_b + n_bank - 3)

    def remote(src, dst, sends, recvs, k, peer):
        return pltpu.make_async_remote_copy(
            src_ref=src,
            dst_ref=dst,
            send_sem=sends.at[k],
            recv_sem=recvs.at[k],
            device_id={"gal": peer},
            device_id_type=MESH,
        )

    def bank_first(k):
        return remote(
            bankq_hbm, bank_all.at[0, n_a - k], bank_send.at[0], bank_recv.at[0], k, along_a(k)
        )

    def test_first(k):
        return remote(
            testq_hbm, test_row.at[me_a], test_send.at[0], test_recv.at[0], k, along_a(k)
        )

    reach = [k for k in far_first(n_b) if min(k, n_b - k) <= 2]

    def bank_second(k):
        return remote(
            bank_all.at[0], bank_all.at[place_of[n_b - k]],
            bank_send.at[1], bank_recv.at[1], k, along_b(k),
        )

    passes = []
    if n_b == 8:
        passes = [(2, 1, 0, n_a, 1), (6, 7, 0, n_a, 7), (2, 2, 0, n_a // 2, 2), (6, 6, n_a // 2, n_a, 6)]

    def bank_third(source, step, low, high, k):
        part = pl.ds(low, high - low)
        return remote(
            bank_all.at[place_of[n_b - source], part],
            bank_all.at[place_of[(2 * n_b - source - step) % n_b], part],
            bank_send.at[2], bank_recv.at[2], k, along_b(step),
        )

    def test_second(k):
        return remote(
            test_out.at[(me_b + k) % n_b], test_in.at[me_b],
            test_send.at[1], test_recv.at[1], k, along_b(k),
        )

    for k in far_first(n_a):
        bank_first(k).start()
    for k in far_first(n_a):
        test_first(k).start()

    ones = jnp.ones((8, width), jnp.bfloat16)

    def norms(n, carry):
        load(n).wait()
        part = pl.ds(pl.multiple_of(n * chunk, chunk), chunk)
        values = gal[part, :].astype(jnp.float32)
        squares = values * values
        high = squares.astype(jnp.bfloat16)
        low = (squares - high.astype(jnp.float32)).astype(jnp.bfloat16)
        total = matmul(ones, high, NT) + matmul(ones, low, NT)
        gscale[:, part] = lax.rsqrt(total[0:1] + epsilon)
        return carry

    lax.fori_loop(0, chunks, norms, 0, unroll=True)

    fetches[0].wait()
    for k in far_first(n_a):
        bank_first(k).wait_recv()
    for k in reach:
        bank_second(k).start()

    for fetch in fetches[1:]:
        fetch.wait()
    slots = SLOTS * n_gal
    own_rows = testq_hbm.shape[0]
    queries = n_gal * own_rows
    slabs = slabs_ref[...]
    offsets = offsets_ref[...].astype(jnp.float32)
    n_list = slabs_ref.shape[0]
    slot_row = lax.broadcasted_iota(jnp.int32, (slots, queries), 0)
    query_col = lax.broadcasted_iota(jnp.int32, (slots, queries), 1)
    row_a = slot_row // SLOTS % n_a
    row_b = slot_row // (SLOTS * n_a)

    def rank_of(hits):
        lane = lax.broadcasted_iota(jnp.int32, hits.shape, 1) % own_rows
        rank = jnp.zeros(hits.shape, jnp.float32)
        for k in range(1, own_rows):
            rank = rank + jnp.where(lane >= k, pltpu.roll(hits, k, 1), 0.0)
        return rank

    target = device(me_a, row_b)
    listed = jnp.zeros((slots, queries), jnp.float32)
    for s in range(n_list):
        listed = listed + jnp.where(slabs[s : s + 1] == target, 1.0, 0.0)
    forward = jnp.where(
        (query_col // own_rows == device(row_a, me_b))
        & (listed > 0.5)
        & (rank_of(listed).astype(jnp.int32) == slot_row % SLOTS),
        1.0,
        0.0,
    )
    ring_row = lax.broadcasted_iota(jnp.int32, (n_a * own_rows, queries), 0)
    ring_col = lax.broadcasted_iota(jnp.int32, (n_a * own_rows, queries), 1)
    fold = jnp.where(
        ring_col == device(ring_row // own_rows, me_b) * own_rows + ring_row % own_rows, 1.0, 0.0
    )
    forward = matmul(forward.astype(jnp.bfloat16), fold.astype(jnp.bfloat16), NT)
    for k in far_first(n_a):
        test_first(k).wait_recv()
    ring_rows = test_row[...].reshape(n_a * own_rows, width)
    packed = matmul(forward.astype(jnp.bfloat16), ring_rows, NN).astype(jnp.bfloat16)
    test_out[...] = packed.reshape(n_b, SLOTS * n_a, width)
    test_in[me_b] = test_out[me_b]

    named = slabs == me_g
    hit = jnp.sum(jnp.where(named, 1.0, 0.0), axis=0, keepdims=True)
    place = jnp.sum(jnp.where(named, offsets, 0.0), axis=0, keepdims=True)
    rank = rank_of(jnp.broadcast_to(hit, (8, queries)))[0:1]
    pick = jnp.where(
        (query_col // own_rows == device(row_a, row_b))
        & (hit > 0.5)
        & (rank.astype(jnp.int32) == slot_row % SLOTS),
        1.0,
        0.0,
    )
    slot_hit = jnp.sum(pick, axis=1, keepdims=True)
    slot_place = jnp.sum(pick * place, axis=1, keepdims=True)
    slot_block = jnp.where(slot_hit > 0.5, slot_place, -1.0).astype(jnp.int32)

    for k in reach:
        bank_second(k).wait_recv()
        for third in passes:
            if third[0] == k:
                bank_third(*third).start()
    for k in far_first(n_b):
        test_second(k).start()

    def column_sums(low, high, write):
        portion = bank_all[low:high].reshape((high - low) * n_a * bankq_hbm.shape[0], width)
        values = portion.astype(jnp.float32)
        bank_scale = (SHARPNESS * LOG2E) * lax.rsqrt(
            jnp.sum(values * values, axis=1, keepdims=True) + epsilon
        )

        def one(n, carry):
            part = pl.ds(pl.multiple_of(n * chunk, chunk), chunk)
            s = matmul(portion, gal[part, :], NT)
            e = jnp.exp2(s * bank_scale * gscale[:, part])
            write(part, jnp.sum(e, axis=0, keepdims=True))
            return carry

        lax.fori_loop(0, chunks, one, 0, unroll=True)

    def near(part, value):
        near_sums[:, part] = value

    def both(part, value):
        sums[me_bank, :, part] = near_sums[:, part] + value

    column_sums(0, n_b // 2, near)
    for third in passes:
        bank_third(*third).wait_recv()
    column_sums(n_b // 2, n_b, both)

    def share(k):
        return pltpu.make_async_remote_copy(
            src_ref=sums.at[me_bank],
            dst_ref=sums.at[me_bank],
            send_sem=sum_send.at[k],
            recv_sem=sum_recv.at[k],
            device_id={"bank": (me_bank + k) % n_bank},
            device_id_type=MESH,
        )

    for k in far_first(n_bank):
        share(k).start()

    for k in far_first(n_b):
        test_second(k).wait_recv()
    packed = test_in[...].reshape(slots, width)
    asked = packed.astype(jnp.float32)
    test_scale = (SHARPNESS * LOG2E) * lax.rsqrt(
        jnp.sum(asked * asked, axis=1, keepdims=True) + epsilon
    )

    def raw_weights(n, carry):
        part = pl.ds(pl.multiple_of(n * chunk, chunk), chunk)
        s = matmul(packed, gal[part, :], NT)
        e = jnp.exp2(s * test_scale * gscale[:, part])
        block = n * (chunk // BLOCK) + (
            lax.broadcasted_iota(jnp.int32, (slots, chunk), 1) // BLOCK
        )
        scores[:, part] = jnp.where(block == slot_block, e, 0.0)
        return carry

    lax.fori_loop(0, chunks, raw_weights, 0, unroll=True)

    for k in range(1, n_bank):
        share(k).wait_recv()
    inverse = 1.0 / jnp.sum(sums[...], axis=0)

    weights = scores[...] * inverse
    total = jnp.sum(weights, axis=1, keepdims=True)
    numer = matmul(weights.astype(jnp.bfloat16), gal[...], NN)
    total_high = total.astype(jnp.bfloat16).astype(jnp.float32)
    lanes = lax.broadcasted_iota(jnp.int32, (slots, EXTRA), 1)
    extra = jnp.where(lanes == 0, total_high, jnp.where(lanes == 1, total - total_high, 0.0))
    message = jnp.concatenate([numer, extra], axis=1).astype(jnp.bfloat16)
    back_out[...] = message.reshape(n_gal, SLOTS, width + EXTRA)

    def give(k, carry):
        step_a, step_b = k // n_b, k % n_b
        shift_a = n_a // 2 + jnp.where(step_a % 2 == 1, 1, n_a - 1) * ((step_a + 1) // 2)
        shift_b = n_b // 2 + jnp.where(step_b % 2 == 1, 1, n_b - 1) * ((step_b + 1) // 2)
        peer_a, peer_b = (me_a + shift_a) % n_a, (me_b + shift_b) % n_b
        pltpu.make_async_remote_copy(
            src_ref=back_out.at[peer_b * n_a + peer_a],
            dst_ref=back_in.at[me_b * n_a + me_a],
            send_sem=back_send,
            recv_sem=back_recv,
            device_id={"gal": device(peer_a, peer_b)},
            device_id_type=MESH,
        ).start()
        return carry

    lax.fori_loop(0, n_gal - 1, give, 0)
    back_in[me_b * n_a + me_a] = back_out[me_b * n_a + me_a]

    slab_of = device(row_a, row_b)
    lists = jnp.zeros((slots, queries), jnp.float32)
    for s in range(n_list):
        lists = lists + jnp.where(slabs[s : s + 1] == slab_of, 1.0, 0.0)
    own_row = lax.broadcasted_iota(jnp.int32, (8, queries), 0)
    own_col = lax.broadcasted_iota(jnp.int32, (8, queries), 1)
    mine = jnp.where(
        (own_col == me_g * own_rows + own_row) & (own_row < own_rows), 1.0, 0.0
    )
    mine_lists = matmul(mine.astype(jnp.bfloat16), lists.astype(jnp.bfloat16), NT)
    before = jnp.where(
        lax.broadcasted_iota(jnp.int32, (8, 8), 1) < lax.broadcasted_iota(jnp.int32, (8, 8), 0),
        1.0,
        0.0,
    )
    mine_rank = matmul(before, mine_lists, NN)
    slot_col = lax.broadcasted_iota(jnp.int32, (8, slots), 1)
    take = jnp.where(
        (mine_lists > 0.5) & ((mine_rank + 0.5).astype(jnp.int32) == slot_col % SLOTS), 1.0, 0.0
    )

    everyone = pltpu.make_async_remote_copy(
        src_ref=back_out.at[pl.ds(0, n_gal - 1)],
        dst_ref=back_in.at[pl.ds(0, n_gal - 1)],
        send_sem=back_send,
        recv_sem=back_recv,
        device_id={"gal": along_a(1)},
        device_id_type=MESH,
    )
    everyone.wait_recv()
    got = back_in[...].reshape(slots, width + EXTRA)
    answer = matmul(take.astype(jnp.bfloat16), got, NN)
    bottom = answer[:, width : width + 1] + answer[:, width + 1 : width + 2]
    out_ref[...] = (answer[:, :width] / bottom)[:own_rows]

    everyone.wait_send()
    for k in range(1, n_bank):
        share(k).wait_send()
    for k in far_first(n_a):
        bank_first(k).wait_send()
        test_first(k).wait_send()
    for k in reach:
        bank_second(k).wait_send()
    for third in passes:
        bank_third(*third).wait_send()
    for k in far_first(n_b):
        test_second(k).wait_send()


def body(n_bank, n_a, n_b, chunk, bank_queries, gallery, test_queries, test_slabs, test_offsets):
    rows, width = gallery.shape
    n_gal = n_a * n_b
    own_bank, own_test = bank_queries.shape[0], test_queries.shape[0]
    slots = SLOTS * n_gal
    vmem = pl.BlockSpec(memory_space=pltpu.VMEM)
    return pl.pallas_call(
        functools.partial(kernel, n_bank, n_a, n_b, chunk),
        out_shape=jax.ShapeDtypeStruct((own_test, width), jnp.float32),
        in_specs=[pl.BlockSpec(memory_space=pltpu.HBM)] * 5,
        out_specs=vmem,
        scratch_shapes=[
            pltpu.VMEM(test_slabs.T.shape, jnp.int32),
            pltpu.VMEM(test_slabs.T.shape, jnp.int32),
            pltpu.VMEM((rows, width), jnp.bfloat16),
            pltpu.VMEM((n_b, n_a, own_bank, width), jnp.bfloat16),
            pltpu.VMEM((n_a, own_test, width), jnp.bfloat16),
            pltpu.VMEM((n_b, SLOTS * n_a, width), jnp.bfloat16),
            pltpu.VMEM((n_b, SLOTS * n_a, width), jnp.bfloat16),
            pltpu.VMEM((1, rows), jnp.float32),
            pltpu.VMEM((1, rows), jnp.float32),
            pltpu.VMEM((n_bank, 1, rows), jnp.float32),
            pltpu.VMEM((slots, rows), jnp.float32),
            pltpu.VMEM((n_gal, SLOTS, width + EXTRA), jnp.bfloat16),
            pltpu.VMEM((n_gal, SLOTS, width + EXTRA), jnp.bfloat16),
            pltpu.SemaphoreType.DMA((4,)),
            pltpu.SemaphoreType.DMA((rows // chunk,)),
            pltpu.SemaphoreType.DMA((3, 8)),
            pltpu.SemaphoreType.DMA((3, 8)),
            pltpu.SemaphoreType.DMA((2, 8)),
            pltpu.SemaphoreType.DMA((2, 8)),
            pltpu.SemaphoreType.DMA((n_bank,)),
            pltpu.SemaphoreType.DMA((n_bank,)),
            pltpu.SemaphoreType.DMA,
            pltpu.SemaphoreType.DMA,
        ],
        compiler_params=pltpu.CompilerParams(
            collective_id=0, has_side_effects=True, vmem_limit_bytes=60 * 1024 * 1024
        ),
    )(bank_queries, test_queries, test_slabs.T, test_offsets.T, gallery)


def solution(mesh):
    n_bank, n_gal = mesh.shape["bank"], mesh.shape["gal"]
    side = int(n_gal**0.5)
    run = functools.partial(body, n_bank, side, side, 512)
    in_specs = (
        P(("bank", "gal"), None),
        P("gal", None),
        P(("bank", "gal"), None),
        P("bank", None),
        P("bank", None),
    )
    out_specs = P(("bank", "gal"), None)
    return jax.shard_map(run, mesh=mesh, in_specs=in_specs, out_specs=out_specs, check_vma=False)
```

```python
import functools
import jax
import jax.numpy as jnp
from jax import lax
from jax.experimental import pallas as pl
from jax.experimental.pallas import tpu as pltpu
from jax.sharding import PartitionSpec as P

BLOCK = 128
SLOTS = 2
EXTRA = 128
SHARPNESS = 20.0
LOG2E = 1.4426950408889634
epsilon = 1e-06
MESH = pl.DeviceIdType.MESH
NT = (((1,), (1,)), ((), ()))
NN = (((1,), (0,)), ((), ()))


def matmul(left, right, dims):
    return lax.dot_general(left, right, dims, preferred_element_type=jnp.float32)


def kernel(
    n_bank, n_a, n_b, chunk,
    bankq_hbm, testq_hbm, slabs_hbm, offsets_hbm, gal_hbm,
    out_ref,
    slabs_ref, offsets_ref, gal, bank_all, test_row, test_out, test_in,
    gscale, near_sums, sums, scores, back_out, back_in,
    own_sem, gal_sem, bank_send, bank_recv, test_send, test_recv,
    sum_send, sum_recv, back_send, back_recv,
):
    n_gal = n_a * n_b
    rows, width = gal.shape
    chunks = rows // chunk
    me_bank = lax.axis_index("bank")
    me_g = lax.axis_index("gal")
    core = me_bank % 2
    me_a = jnp.where(core == 0, me_g % n_a, me_g // n_b)
    me_b = jnp.where(core == 0, me_g // n_a, me_g % n_b)

    def device(a, b):
        return jnp.where(core == 0, b * n_a + a, a * n_b + b)

    def along_a(k):
        return device((me_a + k) % n_a, me_b)

    def along_b(k):
        return device(me_a, (me_b + k) % n_b)

    def far_first(n):
        return sorted(range(1, n), key=lambda k: -min(k, n - k))

    def load(n):
        part = pl.ds(n * chunk, chunk)
        return pltpu.make_async_copy(gal_hbm.at[part], gal.at[part], gal_sem.at[n])

    barrier = pltpu.get_barrier_semaphore()
    for along, n in ((along_a, n_a), (along_b, n_b)):
        for k in far_first(n):
            pl.semaphore_signal(barrier, inc=1, device_id={"gal": along(k)}, device_id_type=MESH)
    for k in far_first(n_bank):
        pl.semaphore_signal(
            barrier, inc=1, device_id={"bank": (me_bank + k) % n_bank}, device_id_type=MESH
        )
    order = sorted(range(n_b), key=lambda k: (min(k, n_b - k), k))
    place_of = {k: p for p, k in enumerate(order)}
    fetches = [
        pltpu.make_async_copy(bankq_hbm, bank_all.at[0, 0], own_sem.at[0]),
        pltpu.make_async_copy(testq_hbm, test_row.at[me_a], own_sem.at[1]),
        pltpu.make_async_copy(slabs_hbm, slabs_ref, own_sem.at[2]),
        pltpu.make_async_copy(offsets_hbm, offsets_ref, own_sem.at[3]),
    ]
    for fetch in fetches:
        fetch.start()
    pl.semaphore_wait(barrier, n_a + n_b + n_bank - 3)

    def remote(src, dst, sends, recvs, k, peer):
        return pltpu.make_async_remote_copy(
            src_ref=src,
            dst_ref=dst,
            send_sem=sends.at[k],
            recv_sem=recvs.at[k],
            device_id={"gal": peer},
            device_id_type=MESH,
        )

    def bank_first(k):
        return remote(
            bankq_hbm, bank_all.at[0, n_a - k], bank_send.at[0], bank_recv.at[0], k, along_a(k)
        )

    def test_first(k):
        return remote(
            testq_hbm, test_row.at[me_a], test_send.at[0], test_recv.at[0], k, along_a(k)
        )

    reach = [2, 6, 3, 5, 1, 7] if n_b == 8 else far_first(n_b)

    def bank_second(k):
        return remote(
            bank_all.at[0], bank_all.at[place_of[n_b - k]],
            bank_send.at[1], bank_recv.at[1], k, along_b(k),
        )

    passes = []
    if n_b == 8:
        passes = [(2, 2, 0, n_a // 2, 2), (6, 6, n_a // 2, n_a, 6)]

    def bank_third(source, step, low, high, k):
        part = pl.ds(low, high - low)
        return remote(
            bank_all.at[place_of[n_b - source], part],
            bank_all.at[place_of[(2 * n_b - source - step) % n_b], part],
            bank_send.at[2], bank_recv.at[2], k, along_b(step),
        )

    def test_second(k):
        return remote(
            test_out.at[(me_b + k) % n_b], test_in.at[me_b],
            test_send.at[1], test_recv.at[1], k, along_b(k),
        )

    for k in far_first(n_a):
        bank_first(k).start()
    for k in far_first(n_a):
        test_first(k).start()
    for n in range(chunks):
        load(n).start()

    for fetch in fetches[1:]:
        fetch.wait()
    slots = SLOTS * n_gal
    own_rows = testq_hbm.shape[0]
    queries = n_gal * own_rows
    slabs = slabs_ref[...]
    offsets = offsets_ref[...].astype(jnp.float32)
    n_list = slabs_ref.shape[0]
    slot_row = lax.broadcasted_iota(jnp.int32, (slots, queries), 0)
    query_col = lax.broadcasted_iota(jnp.int32, (slots, queries), 1)
    row_a = slot_row // SLOTS % n_a
    row_b = slot_row // (SLOTS * n_a)

    def rank_of(hits):
        lane = lax.broadcasted_iota(jnp.int32, hits.shape, 1) % own_rows
        rank = jnp.zeros(hits.shape, jnp.float32)
        for k in range(1, own_rows):
            rank = rank + jnp.where(lane >= k, pltpu.roll(hits, k, 1), 0.0)
        return rank

    target = device(me_a, row_b)
    listed = jnp.zeros((slots, queries), jnp.float32)
    for s in range(n_list):
        listed = listed + jnp.where(slabs[s : s + 1] == target, 1.0, 0.0)
    forward = jnp.where(
        (query_col // own_rows == device(row_a, me_b))
        & (listed > 0.5)
        & (rank_of(listed).astype(jnp.int32) == slot_row % SLOTS),
        1.0,
        0.0,
    )
    ring_row = lax.broadcasted_iota(jnp.int32, (n_a * own_rows, queries), 0)
    ring_col = lax.broadcasted_iota(jnp.int32, (n_a * own_rows, queries), 1)
    fold = jnp.where(
        ring_col == device(ring_row // own_rows, me_b) * own_rows + ring_row % own_rows, 1.0, 0.0
    )
    forward = matmul(forward.astype(jnp.bfloat16), fold.astype(jnp.bfloat16), NT)
    fetches[0].wait()
    for k in far_first(n_a):
        bank_first(k).wait_recv()
    for k in reach:
        bank_second(k).start()

    for k in far_first(n_a):
        test_first(k).wait_recv()
    ring_rows = test_row[...].reshape(n_a * own_rows, width)
    packed = matmul(forward.astype(jnp.bfloat16), ring_rows, NN).astype(jnp.bfloat16)
    test_out[...] = packed.reshape(n_b, SLOTS * n_a, width)
    test_in[me_b] = test_out[me_b]


    ones = jnp.ones((8, width), jnp.bfloat16)

    def norms(n, carry):
        load(n).wait()
        part = pl.ds(pl.multiple_of(n * chunk, chunk), chunk)
        values = gal[part, :].astype(jnp.float32)
        squares = values * values
        high = squares.astype(jnp.bfloat16)
        low = (squares - high.astype(jnp.float32)).astype(jnp.bfloat16)
        total = matmul(ones, high, NT) + matmul(ones, low, NT)
        gscale[:, part] = lax.rsqrt(total[0:1] + epsilon)
        return carry

    lax.fori_loop(0, chunks, norms, 0, unroll=True)

    sources = [third[0] for third in passes]
    for third in passes:
        bank_second(third[0]).wait_recv()
        bank_third(*third).start()

    for k in far_first(n_b):
        test_second(k).start()

    named = slabs == me_g
    hit = jnp.sum(jnp.where(named, 1.0, 0.0), axis=0, keepdims=True)
    place = jnp.sum(jnp.where(named, offsets, 0.0), axis=0, keepdims=True)
    rank = rank_of(jnp.broadcast_to(hit, (8, queries)))[0:1]
    pick = jnp.where(
        (query_col // own_rows == device(row_a, row_b))
        & (hit > 0.5)
        & (rank.astype(jnp.int32) == slot_row % SLOTS),
        1.0,
        0.0,
    )
    slot_hit = jnp.sum(pick, axis=1, keepdims=True)
    slot_place = jnp.sum(pick * place, axis=1, keepdims=True)
    slot_block = jnp.where(slot_hit > 0.5, slot_place, -1.0).astype(jnp.int32)

    def column_sums(low, high, write):
        portion = bank_all[low:high].reshape((high - low) * n_a * bankq_hbm.shape[0], width)
        values = portion.astype(jnp.float32)
        bank_scale = (SHARPNESS * LOG2E) * lax.rsqrt(
            jnp.sum(values * values, axis=1, keepdims=True) + epsilon
        )

        def one(n, carry):
            part = pl.ds(pl.multiple_of(n * chunk, chunk), chunk)
            s = matmul(portion, gal[part, :], NT)
            e = jnp.exp2(s * bank_scale * gscale[:, part])
            write(part, jnp.sum(e, axis=0, keepdims=True))
            return carry

        lax.fori_loop(0, chunks, one, 0, unroll=True)

    def first_pass(part, value):
        near_sums[:, part] = value

    def both(part, value):
        sums[me_bank, :, part] = near_sums[:, part] + value

    early = [n_b - k for k in order[1 : n_b // 2]]
    for k in early:
        if k not in sources:
            bank_second(k).wait_recv()
    column_sums(0, n_b // 2, first_pass)
    for k in reach:
        if k not in early and k not in sources:
            bank_second(k).wait_recv()
    for third in passes:
        bank_third(*third).wait_recv()
    column_sums(n_b // 2, n_b, both)

    def share(k):
        return pltpu.make_async_remote_copy(
            src_ref=sums.at[me_bank],
            dst_ref=sums.at[me_bank],
            send_sem=sum_send.at[k],
            recv_sem=sum_recv.at[k],
            device_id={"bank": (me_bank + k) % n_bank},
            device_id_type=MESH,
        )

    for k in far_first(n_bank):
        share(k).start()

    for k in far_first(n_b):
        test_second(k).wait_recv()
    packed = test_in[...].reshape(slots, width)
    asked = packed.astype(jnp.float32)
    test_scale = (SHARPNESS * LOG2E) * lax.rsqrt(
        jnp.sum(asked * asked, axis=1, keepdims=True) + epsilon
    )

    def raw_weights(n, carry):
        part = pl.ds(pl.multiple_of(n * chunk, chunk), chunk)
        s = matmul(packed, gal[part, :], NT)
        e = jnp.exp2(s * test_scale * gscale[:, part])
        block = n * (chunk // BLOCK) + (
            lax.broadcasted_iota(jnp.int32, (slots, chunk), 1) // BLOCK
        )
        scores[:, part] = jnp.where(block == slot_block, e, 0.0)
        return carry

    lax.fori_loop(0, chunks, raw_weights, 0, unroll=True)

    for k in range(1, n_bank):
        share(k).wait_recv()
    inverse = 1.0 / jnp.sum(sums[...], axis=0)

    weights = scores[...] * inverse
    total = jnp.sum(weights, axis=1, keepdims=True)
    numer = matmul(weights.astype(jnp.bfloat16), gal[...], NN)
    total_high = total.astype(jnp.bfloat16).astype(jnp.float32)
    lanes = lax.broadcasted_iota(jnp.int32, (slots, EXTRA), 1)
    extra = jnp.where(lanes == 0, total_high, jnp.where(lanes == 1, total - total_high, 0.0))
    message = jnp.concatenate([numer, extra], axis=1).astype(jnp.bfloat16)
    back_out[...] = message.reshape(n_gal, SLOTS, width + EXTRA)

    def near(k, n):
        return min(k, n - k)

    steps = [(a, b) for a in range(n_a) for b in range(n_b) if (a, b) != (0, 0)]
    for step_a, step_b in sorted(steps, key=lambda p: -near(p[0], n_a) - near(p[1], n_b)):
        peer_a, peer_b = (me_a + step_a) % n_a, (me_b + step_b) % n_b
        pltpu.make_async_remote_copy(
            src_ref=back_out.at[peer_b * n_a + peer_a],
            dst_ref=back_in.at[me_b * n_a + me_a],
            send_sem=back_send,
            recv_sem=back_recv,
            device_id={"gal": device(peer_a, peer_b)},
            device_id_type=MESH,
        ).start()
    back_in[me_b * n_a + me_a] = back_out[me_b * n_a + me_a]

    slab_of = device(row_a, row_b)
    lists = jnp.zeros((slots, queries), jnp.float32)
    for s in range(n_list):
        lists = lists + jnp.where(slabs[s : s + 1] == slab_of, 1.0, 0.0)
    own_row = lax.broadcasted_iota(jnp.int32, (8, queries), 0)
    own_col = lax.broadcasted_iota(jnp.int32, (8, queries), 1)
    mine = jnp.where(
        (own_col == me_g * own_rows + own_row) & (own_row < own_rows), 1.0, 0.0
    )
    mine_lists = matmul(mine.astype(jnp.bfloat16), lists.astype(jnp.bfloat16), NT)
    before = jnp.where(
        lax.broadcasted_iota(jnp.int32, (8, 8), 1) < lax.broadcasted_iota(jnp.int32, (8, 8), 0),
        1.0,
        0.0,
    )
    mine_rank = matmul(before, mine_lists, NN)
    slot_col = lax.broadcasted_iota(jnp.int32, (8, slots), 1)
    take = jnp.where(
        (mine_lists > 0.5) & ((mine_rank + 0.5).astype(jnp.int32) == slot_col % SLOTS), 1.0, 0.0
    )

    everyone = pltpu.make_async_remote_copy(
        src_ref=back_out.at[pl.ds(0, n_gal - 1)],
        dst_ref=back_in.at[pl.ds(0, n_gal - 1)],
        send_sem=back_send,
        recv_sem=back_recv,
        device_id={"gal": along_a(1)},
        device_id_type=MESH,
    )
    everyone.wait_recv()
    got = back_in[...].reshape(slots, width + EXTRA)
    answer = matmul(take.astype(jnp.bfloat16), got, NN)
    bottom = answer[:, width : width + 1] + answer[:, width + 1 : width + 2]
    out_ref[...] = (answer[:, :width] / bottom)[:own_rows]

    everyone.wait_send()
    for k in range(1, n_bank):
        share(k).wait_send()
    for k in far_first(n_a):
        bank_first(k).wait_send()
        test_first(k).wait_send()
    for k in reach:
        bank_second(k).wait_send()
    for third in passes:
        bank_third(*third).wait_send()
    for k in far_first(n_b):
        test_second(k).wait_send()


def body(n_bank, n_a, n_b, chunk, bank_queries, gallery, test_queries, test_slabs, test_offsets):
    rows, width = gallery.shape
    n_gal = n_a * n_b
    own_bank, own_test = bank_queries.shape[0], test_queries.shape[0]
    slots = SLOTS * n_gal
    vmem = pl.BlockSpec(memory_space=pltpu.VMEM)
    return pl.pallas_call(
        functools.partial(kernel, n_bank, n_a, n_b, chunk),
        out_shape=jax.ShapeDtypeStruct((own_test, width), jnp.float32),
        in_specs=[pl.BlockSpec(memory_space=pltpu.HBM)] * 5,
        out_specs=vmem,
        scratch_shapes=[
            pltpu.VMEM(test_slabs.T.shape, jnp.int32),
            pltpu.VMEM(test_slabs.T.shape, jnp.int32),
            pltpu.VMEM((rows, width), jnp.bfloat16),
            pltpu.VMEM((n_b, n_a, own_bank, width), jnp.bfloat16),
            pltpu.VMEM((n_a, own_test, width), jnp.bfloat16),
            pltpu.VMEM((n_b, SLOTS * n_a, width), jnp.bfloat16),
            pltpu.VMEM((n_b, SLOTS * n_a, width), jnp.bfloat16),
            pltpu.VMEM((1, rows), jnp.float32),
            pltpu.VMEM((1, rows), jnp.float32),
            pltpu.VMEM((n_bank, 1, rows), jnp.float32),
            pltpu.VMEM((slots, rows), jnp.float32),
            pltpu.VMEM((n_gal, SLOTS, width + EXTRA), jnp.bfloat16),
            pltpu.VMEM((n_gal, SLOTS, width + EXTRA), jnp.bfloat16),
            pltpu.SemaphoreType.DMA((4,)),
            pltpu.SemaphoreType.DMA((rows // chunk,)),
            pltpu.SemaphoreType.DMA((3, 8)),
            pltpu.SemaphoreType.DMA((3, 8)),
            pltpu.SemaphoreType.DMA((2, 8)),
            pltpu.SemaphoreType.DMA((2, 8)),
            pltpu.SemaphoreType.DMA((n_bank,)),
            pltpu.SemaphoreType.DMA((n_bank,)),
            pltpu.SemaphoreType.DMA,
            pltpu.SemaphoreType.DMA,
        ],
        compiler_params=pltpu.CompilerParams(
            collective_id=0, has_side_effects=True, vmem_limit_bytes=60 * 1024 * 1024
        ),
    )(bank_queries, test_queries, test_slabs.T, test_offsets.T, gallery)


def solution(mesh):
    n_bank, n_gal = mesh.shape["bank"], mesh.shape["gal"]
    side = int(n_gal**0.5)
    run = functools.partial(body, n_bank, side, side, 512)
    in_specs = (
        P(("bank", "gal"), None),
        P("gal", None),
        P(("bank", "gal"), None),
        P("bank", None),
        P("bank", None),
    )
    out_specs = P(("bank", "gal"), None)
    return jax.shard_map(run, mesh=mesh, in_specs=in_specs, out_specs=out_specs, check_vma=False)
```

```python
import functools
import jax
import jax.numpy as jnp
from jax import lax
from jax.experimental import pallas as pl
from jax.experimental.pallas import tpu as pltpu
from jax.sharding import PartitionSpec as P

BLOCK = 128
SLOTS = 2
EXTRA = 128
SHARPNESS = 20.0
LOG2E = 1.4426950408889634
epsilon = 1e-06
MESH = pl.DeviceIdType.MESH
NT = (((1,), (1,)), ((), ()))
NN = (((1,), (0,)), ((), ()))


def matmul(left, right, dims):
    return lax.dot_general(left, right, dims, preferred_element_type=jnp.float32)


def kernel(
    n_bank, n_a, n_b, chunk,
    bankq_hbm, testq_hbm, slabs_hbm, offsets_hbm, gal_hbm,
    out_ref,
    slabs_ref, offsets_ref, gal, bank_all, test_row, test_out, test_in,
    gscale, near_sums, sums, scores, back_out, back_in,
    own_sem, gal_sem, bank_send, bank_recv, test_send, test_recv,
    sum_send, sum_recv, back_send, back_recv,
):
    n_gal = n_a * n_b
    rows, width = gal.shape
    chunks = rows // chunk
    me_bank = lax.axis_index("bank")
    me_g = lax.axis_index("gal")
    core = me_bank % 2
    me_a = jnp.where(core == 0, me_g % n_a, me_g // n_b)
    me_b = jnp.where(core == 0, me_g // n_a, me_g % n_b)

    def device(a, b):
        return jnp.where(core == 0, b * n_a + a, a * n_b + b)

    def along_a(k):
        return device((me_a + k) % n_a, me_b)

    def along_b(k):
        return device(me_a, (me_b + k) % n_b)

    def far_first(n):
        return sorted(range(1, n), key=lambda k: -min(k, n - k))

    def load(n):
        part = pl.ds(n * chunk, chunk)
        return pltpu.make_async_copy(gal_hbm.at[part], gal.at[part], gal_sem.at[n])

    barrier = pltpu.get_barrier_semaphore()
    greetings = [(min(k, n_a - k), {"gal": along_a(k)}) for k in range(1, n_a)]
    greetings += [(min(k, n_b - k), {"gal": along_b(k)}) for k in range(1, n_b)]
    greetings += [
        (min(k, n_bank - k) // 2, {"bank": (me_bank + k) % n_bank}) for k in range(1, n_bank)
    ]
    for _, partner in sorted(greetings, key=lambda g: -g[0]):
        pl.semaphore_signal(barrier, inc=1, device_id=partner, device_id_type=MESH)
    order = sorted(range(n_b), key=lambda k: (min(k, n_b - k), k))
    place_of = {k: p for p, k in enumerate(order)}
    fetches = [
        pltpu.make_async_copy(bankq_hbm, bank_all.at[0, 0], own_sem.at[0]),
        pltpu.make_async_copy(testq_hbm, test_row.at[me_a], own_sem.at[1]),
        pltpu.make_async_copy(slabs_hbm, slabs_ref, own_sem.at[2]),
        pltpu.make_async_copy(offsets_hbm, offsets_ref, own_sem.at[3]),
    ]
    for fetch in fetches:
        fetch.start()
    pl.semaphore_wait(barrier, n_a + n_b + n_bank - 3)

    def remote(src, dst, sends, recvs, k, peer):
        return pltpu.make_async_remote_copy(
            src_ref=src,
            dst_ref=dst,
            send_sem=sends.at[k],
            recv_sem=recvs.at[k],
            device_id={"gal": peer},
            device_id_type=MESH,
        )

    def bank_first(k):
        return remote(
            bankq_hbm, bank_all.at[0, n_a - k], bank_send.at[0], bank_recv.at[0], k, along_a(k)
        )

    def bank_early(k):
        return remote(
            bankq_hbm, bank_all.at[place_of[n_b - k], 0],
            bank_send.at[4], bank_recv.at[4], k, along_b(k),
        )

    def test_first(k):
        return remote(
            testq_hbm, test_row.at[me_a], test_send.at[0], test_recv.at[0], k, along_a(k)
        )

    middle = n_a // 2
    seconds = [(1, 1, n_a, 1)]
    if n_b == 8:
        seconds = [
            (2, 1, middle, 1), (6, middle, n_a, 1), (3, 1, n_a, 1), (5, 1, n_a, 1),
            (2, middle, n_a, 3), (6, 1, middle, 3), (1, 1, n_a, 1), (7, 1, n_a, 1),
        ]

    def bank_second(k, low, high, lot):
        part = pl.ds(low, high - low)
        return remote(
            bank_all.at[0, part], bank_all.at[place_of[n_b - k], part],
            bank_send.at[lot], bank_recv.at[lot], k, along_b(k),
        )

    passes = []
    if n_b == 8:
        passes = [(2, 2, 1, middle, 2), (6, 6, middle, n_a, 6)]

    def bank_third(source, step, low, high, k):
        part = pl.ds(low, high - low)
        return remote(
            bank_all.at[place_of[n_b - source], part],
            bank_all.at[place_of[(2 * n_b - source - step) % n_b], part],
            bank_send.at[2], bank_recv.at[2], k, along_b(step),
        )

    def test_second(k):
        return remote(
            test_out.at[(me_b + k) % n_b], test_in.at[me_b],
            test_send.at[1], test_recv.at[1], k, along_b(k),
        )

    for k in far_first(n_a):
        bank_first(k).start()
    for k in far_first(n_b):
        bank_early(k).start()
    for k in far_first(n_a):
        test_first(k).start()
    for n in range(chunks):
        load(n).start()

    for fetch in fetches[1:]:
        fetch.wait()
    slots = SLOTS * n_gal
    own_rows = testq_hbm.shape[0]
    queries = n_gal * own_rows
    slabs = slabs_ref[...]
    offsets = offsets_ref[...].astype(jnp.float32)
    n_list = slabs_ref.shape[0]
    slot_row = lax.broadcasted_iota(jnp.int32, (slots, queries), 0)
    query_col = lax.broadcasted_iota(jnp.int32, (slots, queries), 1)
    row_a = slot_row // SLOTS % n_a
    row_b = slot_row // (SLOTS * n_a)

    def rank_of(hits):
        lane = lax.broadcasted_iota(jnp.int32, hits.shape, 1) % own_rows
        rank = jnp.zeros(hits.shape, jnp.float32)
        for k in range(1, own_rows):
            rank = rank + jnp.where(lane >= k, pltpu.roll(hits, k, 1), 0.0)
        return rank

    target = device(me_a, row_b)
    listed = jnp.zeros((slots, queries), jnp.float32)
    for s in range(n_list):
        listed = listed + jnp.where(slabs[s : s + 1] == target, 1.0, 0.0)
    forward = jnp.where(
        (query_col // own_rows == device(row_a, me_b))
        & (listed > 0.5)
        & (rank_of(listed).astype(jnp.int32) == slot_row % SLOTS),
        1.0,
        0.0,
    )
    ring_row = lax.broadcasted_iota(jnp.int32, (n_a * own_rows, queries), 0)
    ring_col = lax.broadcasted_iota(jnp.int32, (n_a * own_rows, queries), 1)
    fold = jnp.where(
        ring_col == device(ring_row // own_rows, me_b) * own_rows + ring_row % own_rows, 1.0, 0.0
    )
    forward = matmul(forward.astype(jnp.bfloat16), fold.astype(jnp.bfloat16), NT)
    fetches[0].wait()
    for k in far_first(n_a):
        bank_first(k).wait_recv()
    for second in seconds:
        bank_second(*second).start()

    for k in far_first(n_a):
        test_first(k).wait_recv()
    ring_rows = test_row[...].reshape(n_a * own_rows, width)
    packed = matmul(forward.astype(jnp.bfloat16), ring_rows, NN).astype(jnp.bfloat16)
    test_out[...] = packed.reshape(n_b, SLOTS * n_a, width)
    test_in[me_b] = test_out[me_b]


    ones = jnp.ones((8, width), jnp.bfloat16)

    def norms(n, carry):
        load(n).wait()
        part = pl.ds(pl.multiple_of(n * chunk, chunk), chunk)
        values = gal[part, :].astype(jnp.float32)
        squares = values * values
        high = squares.astype(jnp.bfloat16)
        low = (squares - high.astype(jnp.float32)).astype(jnp.bfloat16)
        total = matmul(ones, high, NT) + matmul(ones, low, NT)
        gscale[:, part] = lax.rsqrt(total[0:1] + epsilon)
        return carry

    lax.fori_loop(0, chunks // 2, norms, 0, unroll=True)

    waited = seconds[: len(passes)]
    for second, third in zip(waited, passes):
        bank_second(*second).wait_recv()
        bank_third(*third).start()
    for k in far_first(n_b):
        test_second(k).start()

    lax.fori_loop(chunks // 2, chunks, norms, 0, unroll=True)

    named = slabs == me_g
    hit = jnp.sum(jnp.where(named, 1.0, 0.0), axis=0, keepdims=True)
    place = jnp.sum(jnp.where(named, offsets, 0.0), axis=0, keepdims=True)
    rank = rank_of(jnp.broadcast_to(hit, (8, queries)))[0:1]
    pick = jnp.where(
        (query_col // own_rows == device(row_a, row_b))
        & (hit > 0.5)
        & (rank.astype(jnp.int32) == slot_row % SLOTS),
        1.0,
        0.0,
    )
    slot_hit = jnp.sum(pick, axis=1, keepdims=True)
    slot_place = jnp.sum(pick * place, axis=1, keepdims=True)
    slot_block = jnp.where(slot_hit > 0.5, slot_place, -1.0).astype(jnp.int32)

    def column_sums(low, high, write):
        portion = bank_all[low:high].reshape((high - low) * n_a * bankq_hbm.shape[0], width)
        values = portion.astype(jnp.float32)
        bank_scale = (SHARPNESS * LOG2E) * lax.rsqrt(
            jnp.sum(values * values, axis=1, keepdims=True) + epsilon
        )

        def one(n, carry):
            part = pl.ds(pl.multiple_of(n * chunk, chunk), chunk)
            s = matmul(portion, gal[part, :], NT)
            e = jnp.exp2(s * bank_scale * gscale[:, part])
            write(part, jnp.sum(e, axis=0, keepdims=True))
            return carry

        return one

    def first_pass(part, value):
        near_sums[:, part] = value

    def both(part, value):
        sums[me_bank, :, part] = near_sums[:, part] + value

    for k in far_first(n_b):
        bank_early(k).wait_recv()
    early = [n_b - k for k in order[1 : n_b // 2]]
    for second in seconds:
        if second[0] in early and second not in waited:
            bank_second(*second).wait_recv()
    lax.fori_loop(0, chunks, column_sums(0, n_b // 2, first_pass), 0, unroll=True)
    for second in seconds:
        if second[0] not in early and second not in waited:
            bank_second(*second).wait_recv()
    for third in passes:
        bank_third(*third).wait_recv()

    columns = [pl.ds(h * (rows // 2), rows // 2) for h in range(2)]

    def share(k, h):
        return pltpu.make_async_remote_copy(
            src_ref=sums.at[me_bank, :, columns[h]],
            dst_ref=sums.at[me_bank, :, columns[h]],
            send_sem=sum_send.at[h, k],
            recv_sem=sum_recv.at[h, k],
            device_id={"bank": (me_bank + k) % n_bank},
            device_id_type=MESH,
        )

    last_pass = column_sums(n_b // 2, n_b, both)
    for h in range(2):
        lax.fori_loop(h * (chunks // 2), (h + 1) * (chunks // 2), last_pass, 0, unroll=True)
        for k in far_first(n_bank):
            share(k, h).start()

    for k in far_first(n_b):
        test_second(k).wait_recv()
    packed = test_in[...].reshape(slots, width)
    asked = packed.astype(jnp.float32)
    test_scale = (SHARPNESS * LOG2E) * lax.rsqrt(
        jnp.sum(asked * asked, axis=1, keepdims=True) + epsilon
    )

    def raw_weights(n, carry):
        part = pl.ds(pl.multiple_of(n * chunk, chunk), chunk)
        s = matmul(packed, gal[part, :], NT)
        e = jnp.exp2(s * test_scale * gscale[:, part])
        block = n * (chunk // BLOCK) + (
            lax.broadcasted_iota(jnp.int32, (slots, chunk), 1) // BLOCK
        )
        scores[:, part] = jnp.where(block == slot_block, e, 0.0)
        return carry

    lax.fori_loop(0, chunks, raw_weights, 0, unroll=True)

    total = jnp.zeros((slots, 1), jnp.float32)
    numer = jnp.zeros((slots, width), jnp.float32)
    for h in range(2):
        for k in range(1, n_bank):
            share(k, h).wait_recv()
        inverse = 1.0 / jnp.sum(sums[:, :, columns[h]], axis=0)
        weights = scores[:, columns[h]] * inverse
        total = total + jnp.sum(weights, axis=1, keepdims=True)
        numer = numer + matmul(weights.astype(jnp.bfloat16), gal[columns[h], :], NN)
    total_high = total.astype(jnp.bfloat16).astype(jnp.float32)
    lanes = lax.broadcasted_iota(jnp.int32, (slots, EXTRA), 1)
    extra = jnp.where(lanes == 0, total_high, jnp.where(lanes == 1, total - total_high, 0.0))
    message = jnp.concatenate([numer, extra], axis=1).astype(jnp.bfloat16)
    back_out[...] = message.reshape(n_gal, SLOTS, width + EXTRA)

    def near(k, n):
        return min(k, n - k)

    steps = [(a, b) for a in range(n_a) for b in range(n_b) if (a, b) != (0, 0)]
    for step_a, step_b in sorted(steps, key=lambda p: -near(p[0], n_a) - near(p[1], n_b)):
        peer_a, peer_b = (me_a + step_a) % n_a, (me_b + step_b) % n_b
        pltpu.make_async_remote_copy(
            src_ref=back_out.at[peer_b * n_a + peer_a],
            dst_ref=back_in.at[me_b * n_a + me_a],
            send_sem=back_send,
            recv_sem=back_recv,
            device_id={"gal": device(peer_a, peer_b)},
            device_id_type=MESH,
        ).start()
    back_in[me_b * n_a + me_a] = back_out[me_b * n_a + me_a]

    slab_of = device(row_a, row_b)
    lists = jnp.zeros((slots, queries), jnp.float32)
    for s in range(n_list):
        lists = lists + jnp.where(slabs[s : s + 1] == slab_of, 1.0, 0.0)
    own_row = lax.broadcasted_iota(jnp.int32, (8, queries), 0)
    own_col = lax.broadcasted_iota(jnp.int32, (8, queries), 1)
    mine = jnp.where(
        (own_col == me_g * own_rows + own_row) & (own_row < own_rows), 1.0, 0.0
    )
    mine_lists = matmul(mine.astype(jnp.bfloat16), lists.astype(jnp.bfloat16), NT)
    before = jnp.where(
        lax.broadcasted_iota(jnp.int32, (8, 8), 1) < lax.broadcasted_iota(jnp.int32, (8, 8), 0),
        1.0,
        0.0,
    )
    mine_rank = matmul(before, mine_lists, NN)
    slot_col = lax.broadcasted_iota(jnp.int32, (8, slots), 1)
    take = jnp.where(
        (mine_lists > 0.5) & ((mine_rank + 0.5).astype(jnp.int32) == slot_col % SLOTS), 1.0, 0.0
    )

    everyone = pltpu.make_async_remote_copy(
        src_ref=back_out.at[pl.ds(0, n_gal - 1)],
        dst_ref=back_in.at[pl.ds(0, n_gal - 1)],
        send_sem=back_send,
        recv_sem=back_recv,
        device_id={"gal": along_a(1)},
        device_id_type=MESH,
    )
    everyone.wait_recv()
    got = back_in[...].reshape(slots, width + EXTRA)
    answer = matmul(take.astype(jnp.bfloat16), got, NN)
    bottom = answer[:, width : width + 1] + answer[:, width + 1 : width + 2]
    out_ref[...] = (answer[:, :width] / bottom)[:own_rows]

    everyone.wait_send()
    for k in range(1, n_bank):
        for h in range(2):
            share(k, h).wait_send()
    for k in far_first(n_a):
        bank_first(k).wait_send()
        test_first(k).wait_send()
    for k in far_first(n_b):
        bank_early(k).wait_send()
    for second in seconds:
        bank_second(*second).wait_send()
    for third in passes:
        bank_third(*third).wait_send()
    for k in far_first(n_b):
        test_second(k).wait_send()


def body(n_bank, n_a, n_b, chunk, bank_queries, gallery, test_queries, test_slabs, test_offsets):
    rows, width = gallery.shape
    n_gal = n_a * n_b
    own_bank, own_test = bank_queries.shape[0], test_queries.shape[0]
    slots = SLOTS * n_gal
    vmem = pl.BlockSpec(memory_space=pltpu.VMEM)
    return pl.pallas_call(
        functools.partial(kernel, n_bank, n_a, n_b, chunk),
        out_shape=jax.ShapeDtypeStruct((own_test, width), jnp.float32),
        in_specs=[pl.BlockSpec(memory_space=pltpu.HBM)] * 5,
        out_specs=vmem,
        scratch_shapes=[
            pltpu.VMEM(test_slabs.T.shape, jnp.int32),
            pltpu.VMEM(test_slabs.T.shape, jnp.int32),
            pltpu.VMEM((rows, width), jnp.bfloat16),
            pltpu.VMEM((n_b, n_a, own_bank, width), jnp.bfloat16),
            pltpu.VMEM((n_a, own_test, width), jnp.bfloat16),
            pltpu.VMEM((n_b, SLOTS * n_a, width), jnp.bfloat16),
            pltpu.VMEM((n_b, SLOTS * n_a, width), jnp.bfloat16),
            pltpu.VMEM((1, rows), jnp.float32),
            pltpu.VMEM((1, rows), jnp.float32),
            pltpu.VMEM((n_bank, 1, rows), jnp.float32),
            pltpu.VMEM((slots, rows), jnp.float32),
            pltpu.VMEM((n_gal, SLOTS, width + EXTRA), jnp.bfloat16),
            pltpu.VMEM((n_gal, SLOTS, width + EXTRA), jnp.bfloat16),
            pltpu.SemaphoreType.DMA((4,)),
            pltpu.SemaphoreType.DMA((rows // chunk,)),
            pltpu.SemaphoreType.DMA((5, 8)),
            pltpu.SemaphoreType.DMA((5, 8)),
            pltpu.SemaphoreType.DMA((2, 8)),
            pltpu.SemaphoreType.DMA((2, 8)),
            pltpu.SemaphoreType.DMA((2, n_bank)),
            pltpu.SemaphoreType.DMA((2, n_bank)),
            pltpu.SemaphoreType.DMA,
            pltpu.SemaphoreType.DMA,
        ],
        compiler_params=pltpu.CompilerParams(
            collective_id=0, has_side_effects=True, vmem_limit_bytes=60 * 1024 * 1024
        ),
    )(bank_queries, test_queries, test_slabs.T, test_offsets.T, gallery)


def solution(mesh):
    n_bank, n_gal = mesh.shape["bank"], mesh.shape["gal"]
    side = int(n_gal**0.5)
    run = functools.partial(body, n_bank, side, side, 512)
    in_specs = (
        P(("bank", "gal"), None),
        P("gal", None),
        P(("bank", "gal"), None),
        P("bank", None),
        P("bank", None),
    )
    out_specs = P(("bank", "gal"), None)
    return jax.shard_map(run, mesh=mesh, in_specs=in_specs, out_specs=out_specs, check_vma=False)
```

```python
import functools
import jax
import jax.numpy as jnp
from jax import lax
from jax.experimental import pallas as pl
from jax.experimental.pallas import tpu as pltpu
from jax.sharding import PartitionSpec as P

BLOCK = 128
SLOTS = 2
EXTRA = 128
SHARPNESS = 20.0
LOG2E = 1.4426950408889634
epsilon = 1e-06
MESH = pl.DeviceIdType.MESH
NT = (((1,), (1,)), ((), ()))
NN = (((1,), (0,)), ((), ()))


def matmul(left, right, dims):
    return lax.dot_general(left, right, dims, preferred_element_type=jnp.float32)


def kernel(
    n_bank, n_a, n_b, chunk,
    bankq_hbm, testq_hbm, slabs_hbm, offsets_hbm, gal_hbm,
    out_ref,
    slabs_ref, offsets_ref, gal, bank_all, test_row, test_out, test_in,
    gscale, near_sums, sums, scores, back_out, back_in,
    own_sem, gal_sem, bank_send, bank_recv, test_send, test_recv,
    sum_send, sum_recv, back_send, back_recv,
):
    n_gal = n_a * n_b
    rows, width = gal.shape
    chunks = rows // chunk
    me_bank = lax.axis_index("bank")
    me_g = lax.axis_index("gal")
    core = me_bank % 2
    me_a = jnp.where(core == 0, me_g % n_a, me_g // n_b)
    me_b = jnp.where(core == 0, me_g // n_a, me_g % n_b)

    def device(a, b):
        return jnp.where(core == 0, b * n_a + a, a * n_b + b)

    def along_a(k):
        return device((me_a + k) % n_a, me_b)

    def along_b(k):
        return device(me_a, (me_b + k) % n_b)

    def far_first(n):
        return sorted(range(1, n), key=lambda k: -min(k, n - k))

    def load(n):
        part = pl.ds(n * chunk, chunk)
        return pltpu.make_async_copy(gal_hbm.at[part], gal.at[part], gal_sem.at[n])

    barrier = pltpu.get_barrier_semaphore()
    greetings = [(min(k, n_a - k), {"gal": along_a(k)}) for k in range(1, n_a)]
    greetings += [(min(k, n_b - k), {"gal": along_b(k)}) for k in range(1, n_b)]
    greetings += [
        (min(k, n_bank - k) // 2, {"bank": (me_bank + k) % n_bank}) for k in range(1, n_bank)
    ]
    for _, partner in sorted(greetings, key=lambda g: -g[0]):
        pl.semaphore_signal(barrier, inc=1, device_id=partner, device_id_type=MESH)
    order = sorted(range(n_b), key=lambda k: (min(k, n_b - k), k))
    place_of = {k: p for p, k in enumerate(order)}
    fetches = [
        pltpu.make_async_copy(bankq_hbm, bank_all.at[0, 0], own_sem.at[0]),
        pltpu.make_async_copy(testq_hbm, test_row.at[me_a], own_sem.at[1]),
        pltpu.make_async_copy(slabs_hbm, slabs_ref, own_sem.at[2]),
        pltpu.make_async_copy(offsets_hbm, offsets_ref, own_sem.at[3]),
    ]
    for fetch in fetches:
        fetch.start()
    pl.semaphore_wait(barrier, n_a + n_b + n_bank - 3)

    def remote(src, dst, sends, recvs, k, peer):
        return pltpu.make_async_remote_copy(
            src_ref=src,
            dst_ref=dst,
            send_sem=sends.at[k],
            recv_sem=recvs.at[k],
            device_id={"gal": peer},
            device_id_type=MESH,
        )

    def bank_first(k):
        return remote(
            bankq_hbm, bank_all.at[0, n_a - k], bank_send.at[0], bank_recv.at[0], k, along_a(k)
        )

    def bank_early(k):
        return remote(
            bankq_hbm, bank_all.at[place_of[n_b - k], 0],
            bank_send.at[4], bank_recv.at[4], k, along_b(k),
        )

    def test_first(k):
        return remote(
            testq_hbm, test_row.at[me_a], test_send.at[0], test_recv.at[0], k, along_a(k)
        )

    middle = n_a // 2
    seconds = [(1, 1, n_a, 1)]
    if n_b == 8:
        seconds = [
            (2, 1, middle, 1), (6, middle, n_a, 1), (3, 1, n_a, 1), (5, 1, n_a, 1),
            (2, middle, n_a, 3), (6, 1, middle, 3), (1, 1, n_a, 1), (7, 1, n_a, 1),
        ]

    def bank_second(k, low, high, lot):
        part = pl.ds(low, high - low)
        return remote(
            bank_all.at[0, part], bank_all.at[place_of[n_b - k], part],
            bank_send.at[lot], bank_recv.at[lot], k, along_b(k),
        )

    passes = []
    if n_b == 8:
        passes = [(2, 2, 1, middle, 2), (6, 6, middle, n_a, 6)]

    def bank_third(source, step, low, high, k):
        part = pl.ds(low, high - low)
        return remote(
            bank_all.at[place_of[n_b - source], part],
            bank_all.at[place_of[(2 * n_b - source - step) % n_b], part],
            bank_send.at[2], bank_recv.at[2], k, along_b(step),
        )

    def test_second(k):
        return remote(
            test_out.at[(me_b + k) % n_b], test_in.at[me_b],
            test_send.at[1], test_recv.at[1], k, along_b(k),
        )

    for k in far_first(n_a):
        bank_first(k).start()
    for k in far_first(n_b):
        bank_early(k).start()
    for k in far_first(n_a):
        test_first(k).start()
    for n in range(chunks):
        load(n).start()

    for fetch in fetches[1:]:
        fetch.wait()
    slots = SLOTS * n_gal
    own_rows = testq_hbm.shape[0]
    queries = n_gal * own_rows
    slabs = slabs_ref[...]
    offsets = offsets_ref[...].astype(jnp.float32)
    n_list = slabs_ref.shape[0]
    slot_row = lax.broadcasted_iota(jnp.int32, (slots, queries), 0)
    query_col = lax.broadcasted_iota(jnp.int32, (slots, queries), 1)
    row_a = slot_row // SLOTS % n_a
    row_b = slot_row // (SLOTS * n_a)

    def rank_of(hits):
        lane = lax.broadcasted_iota(jnp.int32, hits.shape, 1) % own_rows
        rank = jnp.zeros(hits.shape, jnp.float32)
        for k in range(1, own_rows):
            rank = rank + jnp.where(lane >= k, pltpu.roll(hits, k, 1), 0.0)
        return rank

    target = device(me_a, row_b)
    listed = jnp.zeros((slots, queries), jnp.float32)
    for s in range(n_list):
        listed = listed + jnp.where(slabs[s : s + 1] == target, 1.0, 0.0)
    forward = jnp.where(
        (query_col // own_rows == device(row_a, me_b))
        & (listed > 0.5)
        & (rank_of(listed).astype(jnp.int32) == slot_row % SLOTS),
        1.0,
        0.0,
    )
    ring_row = lax.broadcasted_iota(jnp.int32, (n_a * own_rows, queries), 0)
    ring_col = lax.broadcasted_iota(jnp.int32, (n_a * own_rows, queries), 1)
    fold = jnp.where(
        ring_col == device(ring_row // own_rows, me_b) * own_rows + ring_row % own_rows, 1.0, 0.0
    )
    forward = matmul(forward.astype(jnp.bfloat16), fold.astype(jnp.bfloat16), NT)
    fetches[0].wait()
    for k in far_first(n_a):
        bank_first(k).wait_recv()
    for second in seconds:
        bank_second(*second).start()

    for k in far_first(n_a):
        test_first(k).wait_recv()
    ring_rows = test_row[...].reshape(n_a * own_rows, width)
    packed = matmul(forward.astype(jnp.bfloat16), ring_rows, NN).astype(jnp.bfloat16)
    test_out[...] = packed.reshape(n_b, SLOTS * n_a, width)
    test_in[me_b] = test_out[me_b]


    ones = jnp.ones((8, width), jnp.bfloat16)

    def norms(n, carry):
        load(n).wait()
        part = pl.ds(pl.multiple_of(n * chunk, chunk), chunk)
        values = gal[part, :].astype(jnp.float32)
        squares = values * values
        high = squares.astype(jnp.bfloat16)
        low = (squares - high.astype(jnp.float32)).astype(jnp.bfloat16)
        total = matmul(ones, high, NT) + matmul(ones, low, NT)
        gscale[:, part] = lax.rsqrt(total[0:1] + epsilon)
        return carry

    lax.fori_loop(0, chunks // 2, norms, 0, unroll=True)

    waited = seconds[: len(passes)]
    for second, third in zip(waited, passes):
        bank_second(*second).wait_recv()
        bank_third(*third).start()
    for k in far_first(n_b):
        test_second(k).start()

    lax.fori_loop(chunks // 2, chunks, norms, 0, unroll=True)

    named = slabs == me_g
    hit = jnp.sum(jnp.where(named, 1.0, 0.0), axis=0, keepdims=True)
    place = jnp.sum(jnp.where(named, offsets, 0.0), axis=0, keepdims=True)
    rank = rank_of(jnp.broadcast_to(hit, (8, queries)))[0:1]
    pick = jnp.where(
        (query_col // own_rows == device(row_a, row_b))
        & (hit > 0.5)
        & (rank.astype(jnp.int32) == slot_row % SLOTS),
        1.0,
        0.0,
    )
    slot_hit = jnp.sum(pick, axis=1, keepdims=True)
    slot_place = jnp.sum(pick * place, axis=1, keepdims=True)
    slot_block = jnp.where(slot_hit > 0.5, slot_place, -1.0).astype(jnp.int32)

    def column_sums(low, high, write):
        portion = bank_all[low:high].reshape((high - low) * n_a * bankq_hbm.shape[0], width)
        values = portion.astype(jnp.float32)
        bank_scale = (SHARPNESS * LOG2E) * lax.rsqrt(
            jnp.sum(values * values, axis=1, keepdims=True) + epsilon
        )

        def one(n, carry):
            part = pl.ds(pl.multiple_of(n * chunk, chunk), chunk)
            s = matmul(portion, gal[part, :], NT)
            e = jnp.exp2(s * bank_scale * gscale[:, part])
            write(part, jnp.sum(e, axis=0, keepdims=True))
            return carry

        return one

    def first_pass(part, value):
        near_sums[:, part] = value

    def both(part, value):
        sums[me_bank, :, part] = near_sums[:, part] + value

    for k in far_first(n_b):
        bank_early(k).wait_recv()
    early = [n_b - k for k in order[1 : n_b // 2]]
    for second in seconds:
        if second[0] in early and second not in waited:
            bank_second(*second).wait_recv()
    lax.fori_loop(0, chunks, column_sums(0, n_b // 2, first_pass), 0, unroll=True)
    for second in seconds:
        if second[0] not in early and second not in waited:
            bank_second(*second).wait_recv()
    for third in passes:
        bank_third(*third).wait_recv()

    columns = [pl.ds(0, rows)]

    def share(k, h):
        return pltpu.make_async_remote_copy(
            src_ref=sums.at[me_bank, :, columns[h]],
            dst_ref=sums.at[me_bank, :, columns[h]],
            send_sem=sum_send.at[h, k],
            recv_sem=sum_recv.at[h, k],
            device_id={"bank": (me_bank + k) % n_bank},
            device_id_type=MESH,
        )

    last_pass = column_sums(n_b // 2, n_b, both)
    for h in range(1):
        lax.fori_loop(0, chunks, last_pass, 0, unroll=True)
        for k in far_first(n_bank):
            share(k, h).start()

    for k in far_first(n_b):
        test_second(k).wait_recv()
    packed = test_in[...].reshape(slots, width)
    asked = packed.astype(jnp.float32)
    test_scale = (SHARPNESS * LOG2E) * lax.rsqrt(
        jnp.sum(asked * asked, axis=1, keepdims=True) + epsilon
    )

    def raw_weights(n, carry):
        part = pl.ds(pl.multiple_of(n * chunk, chunk), chunk)
        s = matmul(packed, gal[part, :], NT)
        e = jnp.exp2(s * test_scale * gscale[:, part])
        block = n * (chunk // BLOCK) + (
            lax.broadcasted_iota(jnp.int32, (slots, chunk), 1) // BLOCK
        )
        scores[:, part] = jnp.where(block == slot_block, e, 0.0)
        return carry

    lax.fori_loop(0, chunks, raw_weights, 0, unroll=True)

    total = jnp.zeros((slots, 1), jnp.float32)
    numer = jnp.zeros((slots, width), jnp.float32)
    for h in range(1):
        for k in range(1, n_bank):
            share(k, h).wait_recv()
        inverse = 1.0 / jnp.sum(sums[:, :, columns[h]], axis=0)
        weights = scores[:, columns[h]] * inverse
        total = total + jnp.sum(weights, axis=1, keepdims=True)
        numer = numer + matmul(weights.astype(jnp.bfloat16), gal[columns[h], :], NN)
    total_high = total.astype(jnp.bfloat16).astype(jnp.float32)
    lanes = lax.broadcasted_iota(jnp.int32, (slots, EXTRA), 1)
    extra = jnp.where(lanes == 0, total_high, jnp.where(lanes == 1, total - total_high, 0.0))
    message = jnp.concatenate([numer, extra], axis=1).astype(jnp.bfloat16)
    back_out[...] = message.reshape(n_gal, SLOTS, width + EXTRA)

    def near(k, n):
        return min(k, n - k)

    steps = [(a, b) for a in range(n_a) for b in range(n_b) if (a, b) != (0, 0)]
    for step_a, step_b in sorted(steps, key=lambda p: -near(p[0], n_a) - near(p[1], n_b)):
        peer_a, peer_b = (me_a + step_a) % n_a, (me_b + step_b) % n_b
        pltpu.make_async_remote_copy(
            src_ref=back_out.at[peer_b * n_a + peer_a],
            dst_ref=back_in.at[me_b * n_a + me_a],
            send_sem=back_send,
            recv_sem=back_recv,
            device_id={"gal": device(peer_a, peer_b)},
            device_id_type=MESH,
        ).start()
    back_in[me_b * n_a + me_a] = back_out[me_b * n_a + me_a]

    slab_of = device(row_a, row_b)
    lists = jnp.zeros((slots, queries), jnp.float32)
    for s in range(n_list):
        lists = lists + jnp.where(slabs[s : s + 1] == slab_of, 1.0, 0.0)
    own_row = lax.broadcasted_iota(jnp.int32, (8, queries), 0)
    own_col = lax.broadcasted_iota(jnp.int32, (8, queries), 1)
    mine = jnp.where(
        (own_col == me_g * own_rows + own_row) & (own_row < own_rows), 1.0, 0.0
    )
    mine_lists = matmul(mine.astype(jnp.bfloat16), lists.astype(jnp.bfloat16), NT)
    before = jnp.where(
        lax.broadcasted_iota(jnp.int32, (8, 8), 1) < lax.broadcasted_iota(jnp.int32, (8, 8), 0),
        1.0,
        0.0,
    )
    mine_rank = matmul(before, mine_lists, NN)
    slot_col = lax.broadcasted_iota(jnp.int32, (8, slots), 1)
    take = jnp.where(
        (mine_lists > 0.5) & ((mine_rank + 0.5).astype(jnp.int32) == slot_col % SLOTS), 1.0, 0.0
    )

    everyone = pltpu.make_async_remote_copy(
        src_ref=back_out.at[pl.ds(0, n_gal - 1)],
        dst_ref=back_in.at[pl.ds(0, n_gal - 1)],
        send_sem=back_send,
        recv_sem=back_recv,
        device_id={"gal": along_a(1)},
        device_id_type=MESH,
    )
    everyone.wait_recv()
    got = back_in[...].reshape(slots, width + EXTRA)
    answer = matmul(take.astype(jnp.bfloat16), got, NN)
    bottom = answer[:, width : width + 1] + answer[:, width + 1 : width + 2]
    out_ref[...] = (answer[:, :width] / bottom)[:own_rows]

    everyone.wait_send()
    for k in range(1, n_bank):
        for h in range(1):
            share(k, h).wait_send()
    for k in far_first(n_a):
        bank_first(k).wait_send()
        test_first(k).wait_send()
    for k in far_first(n_b):
        bank_early(k).wait_send()
    for second in seconds:
        bank_second(*second).wait_send()
    for third in passes:
        bank_third(*third).wait_send()
    for k in far_first(n_b):
        test_second(k).wait_send()


def body(n_bank, n_a, n_b, chunk, bank_queries, gallery, test_queries, test_slabs, test_offsets):
    rows, width = gallery.shape
    n_gal = n_a * n_b
    own_bank, own_test = bank_queries.shape[0], test_queries.shape[0]
    slots = SLOTS * n_gal
    vmem = pl.BlockSpec(memory_space=pltpu.VMEM)
    return pl.pallas_call(
        functools.partial(kernel, n_bank, n_a, n_b, chunk),
        out_shape=jax.ShapeDtypeStruct((own_test, width), jnp.float32),
        in_specs=[pl.BlockSpec(memory_space=pltpu.HBM)] * 5,
        out_specs=vmem,
        scratch_shapes=[
            pltpu.VMEM(test_slabs.T.shape, jnp.int32),
            pltpu.VMEM(test_slabs.T.shape, jnp.int32),
            pltpu.VMEM((rows, width), jnp.bfloat16),
            pltpu.VMEM((n_b, n_a, own_bank, width), jnp.bfloat16),
            pltpu.VMEM((n_a, own_test, width), jnp.bfloat16),
            pltpu.VMEM((n_b, SLOTS * n_a, width), jnp.bfloat16),
            pltpu.VMEM((n_b, SLOTS * n_a, width), jnp.bfloat16),
            pltpu.VMEM((1, rows), jnp.float32),
            pltpu.VMEM((1, rows), jnp.float32),
            pltpu.VMEM((n_bank, 1, rows), jnp.float32),
            pltpu.VMEM((slots, rows), jnp.float32),
            pltpu.VMEM((n_gal, SLOTS, width + EXTRA), jnp.bfloat16),
            pltpu.VMEM((n_gal, SLOTS, width + EXTRA), jnp.bfloat16),
            pltpu.SemaphoreType.DMA((4,)),
            pltpu.SemaphoreType.DMA((rows // chunk,)),
            pltpu.SemaphoreType.DMA((5, 8)),
            pltpu.SemaphoreType.DMA((5, 8)),
            pltpu.SemaphoreType.DMA((2, 8)),
            pltpu.SemaphoreType.DMA((2, 8)),
            pltpu.SemaphoreType.DMA((2, n_bank)),
            pltpu.SemaphoreType.DMA((2, n_bank)),
            pltpu.SemaphoreType.DMA,
            pltpu.SemaphoreType.DMA,
        ],
        compiler_params=pltpu.CompilerParams(
            collective_id=0, has_side_effects=True, vmem_limit_bytes=60 * 1024 * 1024
        ),
    )(bank_queries, test_queries, test_slabs.T, test_offsets.T, gallery)


def solution(mesh):
    n_bank, n_gal = mesh.shape["bank"], mesh.shape["gal"]
    side = int(n_gal**0.5)
    run = functools.partial(body, n_bank, side, side, 512)
    in_specs = (
        P(("bank", "gal"), None),
        P("gal", None),
        P(("bank", "gal"), None),
        P("bank", None),
        P("bank", None),
    )
    out_specs = P(("bank", "gal"), None)
    return jax.shard_map(run, mesh=mesh, in_specs=in_specs, out_specs=out_specs, check_vma=False)
```
